32 devices in a mesh: section: 2 (over core), tensor: 4 (over y, x), expert: 4 (over z).
Axes of the slice: x: 2, y: 2, z: 4, core: 2. Of those that a mesh axis runs over, the one named last changes fastest.
Arguments:
- tokens: bfloat16 [2, 4, 256, 768], P(None, 'expert', 'tensor'), may hold values from -6 to 6
- cotangent: float32 [2, 4, 256, 768], P(None, 'expert', 'tensor'), may hold values from -6 to 6
- norm_gains: float32 [2, 2, 768], P('section'), may hold values from 0.5 to 1.5
- norm_shifts: float32 [2, 2, 768], P('section'), may hold values from -3 to 3
- w_qkv: bfloat16 [2, 3, 768, 12, 64], P('section', None, None, 'tensor'), may hold values from -0.21875 to 0.21875
- w_attn_out: bfloat16 [2, 12, 64, 768], P('section', 'tensor'), may hold values from -0.21875 to 0.21875
- w_router: bfloat16 [2, 768, 8], P('section'), may hold values from -0.21875 to 0.21875
- w_in: bfloat16 [2, 8, 768, 3072], P('section', 'expert', None, 'tensor'), may hold values from -0.21875 to 0.21875
- w_out: bfloat16 [2, 8, 3072, 768], P('section', 'expert', 'tensor'), may hold values from -0.3125 to 0.3125
- choices: int32 [2, 2, 4, 256, 2], P('section', None, 'expert'), may hold values from 0 to 7, as said below
- slot_ranks: int32 [2, 2, 4, 256, 2], P('section', None, 'expert'), may hold values from 0 to 64, as said below
Outputs:
- section_out: bfloat16 [2, 2, 4, 256, 768], P('section', None, 'expert', 'tensor')
- input_grad: bfloat16 [2, 2, 4, 256, 768], P('section', None, 'expert', 'tensor')
- grad_norm_gains: float32 [2, 2, 768], P('section')
- grad_norm_shifts: float32 [2, 2, 768], P('section')
- grad_w_qkv: float32 [2, 3, 768, 12, 64], P('section', None, None, 'tensor')
- grad_w_attn_out: float32 [2, 12, 64, 768], P('section', 'tensor')
- grad_w_router: float32 [2, 768, 8], P('section')
- grad_w_in: float32 [2, 8, 768, 3072], P('section', 'expert', None, 'tensor')
- grad_w_out: float32 [2, 8, 3072, 768], P('section', 'expert', 'tensor')
The draws below stay inside these ranges and needn't reach their ends.
Inputs may be any that keep to these rules, and one draw needn't show every extreme that they name: `choices`: the two experts of a token differ. slot_ranks[s, m, row, k] counts the earlier entries that name the same expert in the same block of 256 rows (one index of the expert axis, one section, one micro-batch), where all first choices of the block come before all second choices and rows go in order; it is 64 where that count is 64 or more.
All inputs are finite; a program needn't handle non-finite values.
Results may differ from the reference program's by a relative error of at most 0.025.
Values may be sent and summed in bfloat16 or wider, within the bound.
No kernel may reach another device: no remote copies, remote signals or barrier semaphores. Data moves between devices by JAX's collectives and lax.ppermute only.
A program may use at most 128 MiB of HBM per device.

```python
import jax
import jax.numpy as jnp
from jax import lax

D = 768
HEADS = 12
HEAD_DIM = 64
FF = 3072
EXPERTS = 8
SEQ = 256
IMG_DEV = 1
MICRO = 2
IMGS = 4
CAP = 64
N_EXPERT = 4


def routing_table(key):
    base_key = jax.random.fold_in(key, 11)
    key_one, key_two, key_three, key_four = jax.random.split(base_key, 4)
    block_count = 2 * MICRO * (IMGS // IMG_DEV)
    block_rows = IMG_DEV * SEQ
    first_draw = jax.random.randint(key_one, (block_count, block_rows), 0, EXPERTS)
    second_draw = jax.random.randint(key_two, (block_count, block_rows), 0, EXPERTS)
    lead_expert = first_draw * second_draw // EXPERTS
    offset = jax.random.randint(key_three, (block_count, block_rows), 0, EXPERTS - 1)
    follow_expert = (lead_expert + 1 + offset) % EXPERTS
    relabel = jax.random.permutation(key_four, EXPERTS)
    picked = jnp.stack([relabel[lead_expert], relabel[follow_expert]], axis=1)
    flat_picks = picked.reshape(block_count, 2 * block_rows)
    one_hot = (flat_picks[:, :, None] == jnp.arange(EXPERTS)[None, None, :]).astype(jnp.int32)
    before = jnp.cumsum(one_hot, axis=1) - one_hot
    rank_count = jnp.sum(before * one_hot, axis=2)
    capped = jnp.minimum(rank_count, CAP).reshape(block_count, 2, block_rows)
    out_shape = (2, MICRO, IMGS, SEQ, 2)
    picks_out = jnp.transpose(picked, (0, 2, 1)).reshape(out_shape)
    slots_out = jnp.transpose(capped, (0, 2, 1)).reshape(out_shape)
    return (picks_out.astype(jnp.int32), slots_out.astype(jnp.int32))


def draw_choices(key, part):
    return routing_table(key)[0]


def draw_slot_ranks(key, part):
    return routing_table(key)[1]


def block_levels(own_key, dims, cuts, smallest, high):
    factor_of = 1.0
    for axis_at, parts in cuts:
        draws = jax.random.uniform(jax.random.fold_in(jax.random.fold_in(own_key, 6), axis_at), (parts,), jnp.float32, smallest / len(cuts), high / len(cuts))
        factor_of = factor_of * jnp.repeat(jnp.exp(draws), dims[axis_at] // parts).reshape((-1,) + (1,) * (len(dims) - 1 - axis_at))
    return factor_of


def noise(stream_key, dims, scale, bound, shards=(), held_as=jnp.bfloat16):
    factor_of = block_levels(stream_key, dims, shards, -0.22, 0.18) if shards else 1.0
    drawn = jax.random.normal(stream_key, dims, jnp.float32) * scale * factor_of
    return jnp.minimum(jnp.maximum(drawn, -bound), bound).astype(held_as)


def setup_inputs(seed: int = 0) -> dict:
    keys = jax.random.split(jax.random.key(seed), 12)
    tokens = noise(keys[0], (MICRO, IMGS, SEQ, D), 1.0, 6.0, ((1, 4), (2, 4)))
    cotangent = noise(keys[1], (MICRO, IMGS, SEQ, D), 1.0, 6.0, ((1, 4), (2, 4)), jnp.float32)
    norm_gains = jnp.clip(1.0 + 0.1 * jax.random.normal(keys[2], (2, 2, D), jnp.float32), 0.5, 1.5)
    norm_shifts = noise(keys[3], (2, 2, D), 0.5, 3.0, ((0, 2),), jnp.float32)
    w_qkv = noise(keys[4], (2, 3, D, HEADS, HEAD_DIM), D ** -0.5, 0.21875, ((0, 2), (3, 4)))
    w_attn_out = noise(keys[5], (2, HEADS, HEAD_DIM, D), D ** -0.5, 0.21875, ((0, 2), (1, 4)))
    w_router = noise(keys[6], (2, D, EXPERTS), D ** -0.5, 0.21875, ((0, 2),))
    w_in = noise(keys[7], (2, EXPERTS, D, FF), D ** -0.5, 0.21875, ((0, 2), (1, 4), (3, 4)))
    w_out = noise(keys[8], (2, EXPERTS, FF, D), (FF // 9) ** -0.5, 0.3125, ((0, 2), (1, 4), (2, 4)))
    choices = draw_choices(jax.random.fold_in(keys[11], 71), 0)
    slot_ranks = draw_slot_ranks(jax.random.fold_in(keys[11], 71), 0)
    return {"tokens": tokens, "cotangent": cotangent, "norm_gains": norm_gains, "norm_shifts": norm_shifts, "w_qkv": w_qkv, "w_attn_out": w_attn_out, "w_router": w_router, "w_in": w_in, "w_out": w_out, "choices": choices, "slot_ranks": slot_ranks}


norm_eps = 1e-06
half_root = 0.7071067811865476
tau_root = 0.3989422804014327
highest = lax.Precision.HIGHEST

def widen(low_values):
    return lax.optimization_barrier(low_values).astype(jnp.float32)

def gelu_value(values):
    return 0.5 * values * (1.0 + lax.erf(values * half_root))

def gelu_slope(values):
    return 0.5 * (1.0 + lax.erf(values * half_root)) + values * jnp.exp(-0.5 * values * values) * tau_root

def normalize(values, gain_row, shift_row):
    center = lax.optimization_barrier(jnp.mean(values, axis=-1, keepdims=True))
    deviation = values - center
    factor = lax.rsqrt(lax.optimization_barrier(jnp.mean(deviation * deviation, axis=-1, keepdims=True)) + norm_eps)
    unit_rows = deviation * factor
    return (unit_rows * gain_row + shift_row, unit_rows, factor)

def norm_back(grad_norm, unit_rows, factor, gain_row):
    scaled = grad_norm * gain_row
    return factor * (scaled - lax.optimization_barrier(jnp.mean(scaled, axis=-1, keepdims=True)) - unit_rows * lax.optimization_barrier(jnp.mean(scaled * unit_rows, axis=-1, keepdims=True)))

def expert_apply(packed):
    expert_rows, first_weight, second_weight = packed
    hidden = gelu_value(jnp.dot(expert_rows, first_weight, preferred_element_type=jnp.float32)).astype(jnp.bfloat16)
    return jnp.dot(hidden, second_weight, preferred_element_type=jnp.float32)

def expert_back(packed):
    expert_rows, first_weight, second_weight, out_grad = packed
    inner_rows = jnp.dot(expert_rows, first_weight, preferred_element_type=jnp.float32)
    hidden = gelu_value(inner_rows).astype(jnp.bfloat16)
    hidden_grad = jnp.dot(out_grad, second_weight.T, preferred_element_type=jnp.float32)
    inner_grad = (hidden_grad * gelu_slope(inner_rows)).astype(jnp.bfloat16)
    grad_second = jnp.dot(hidden.T, out_grad, preferred_element_type=jnp.float32)
    grad_first = jnp.dot(expert_rows.T, inner_grad, preferred_element_type=jnp.float32)
    input_part = jnp.dot(inner_grad, first_weight.T, preferred_element_type=jnp.float32)
    return (grad_second, grad_first, input_part)

def layer_forward(block_rows, weights_all, expert_picks, slot_picks):
    gain_rows, shift_rows, w_qkv, w_attn, w_router, w_first, w_second = weights_all
    score_scale = HEAD_DIM ** (-0.5)
    row_count = IMGS * SEQ
    dump_cell = EXPERTS * N_EXPERT * CAP
    start_rows = block_rows.astype(jnp.float32).reshape(row_count, D)
    normed_one, unit_one, factor_one = normalize(start_rows, gain_rows[0], shift_rows[0])
    normed_one = normed_one.astype(jnp.bfloat16)
    qkv_rows = jnp.stack([jnp.dot(normed_one, w_qkv[member].reshape(D, D), preferred_element_type=jnp.float32) for member in range(3)]).astype(jnp.bfloat16)
    qkv_heads = widen(qkv_rows).reshape(3, IMGS, SEQ, HEADS, HEAD_DIM)
    scores = jnp.einsum('ishd,ithd->ihst', qkv_heads[0], qkv_heads[1]) * score_scale
    log_total = jnp.log(lax.optimization_barrier(jnp.sum(jnp.exp(scores), axis=-1, keepdims=True)))
    weights_soft = jnp.exp(scores - log_total).astype(jnp.bfloat16)
    attended = jnp.einsum('ihst,ithd->ishd', widen(weights_soft), qkv_heads[2]).astype(jnp.bfloat16).reshape(row_count, D)
    middle = start_rows + jnp.dot(attended, w_attn.reshape(D, D), preferred_element_type=jnp.float32)
    normed_two, unit_two, factor_two = normalize(middle, gain_rows[1], shift_rows[1])
    normed_two = normed_two.astype(jnp.bfloat16)
    logits = jnp.dot(normed_two, w_router, preferred_element_type=jnp.float32)
    flat_picks = expert_picks.reshape(row_count, 2).astype(jnp.int32)
    flat_slots = slot_picks.reshape(row_count, 2).astype(jnp.int32)
    pick_table = (flat_picks[..., None] == jnp.arange(EXPERTS, dtype=jnp.int32)).astype(jnp.float32)
    chosen = lax.optimization_barrier(jnp.sum(pick_table * logits[:, None, :], axis=-1))
    first_gate = jax.nn.sigmoid(chosen[:, 0] - chosen[:, 1])
    gate_pair = jnp.stack([first_gate, 1.0 - first_gate], axis=-1)
    source = (jnp.arange(row_count, dtype=jnp.int32) // (IMG_DEV * SEQ))[:, None]
    cell_index = jnp.where(flat_slots < CAP, (flat_picks * N_EXPERT + source) * CAP + flat_slots, dump_cell).astype(jnp.int32)
    copies = jnp.broadcast_to(normed_two[:, None, :], (row_count, 2, D)).reshape(-1, D)
    buffer_in = jnp.zeros((dump_cell + 1, D), jnp.bfloat16).at[cell_index.reshape(-1)].set(copies)[:dump_cell].reshape(EXPERTS, N_EXPERT * CAP, D)
    expert_out = lax.map(expert_apply, (buffer_in, w_first, w_second))
    table_out = jnp.concatenate([expert_out.reshape(dump_cell, D), jnp.zeros((1, D), jnp.float32)], axis=0)
    mixed_rows = lax.optimization_barrier(jnp.sum(gate_pair[..., None] * table_out[cell_index], axis=1))
    result = lax.optimization_barrier((middle + mixed_rows).astype(jnp.bfloat16).reshape(block_rows.shape))
    kept_state = (unit_one, factor_one, normed_one, qkv_rows, log_total, attended, unit_two, factor_two, normed_two, pick_table, gate_pair, cell_index, buffer_in, table_out)
    return (result, kept_state)

def layer_backward(grad_rows, weights_all, kept_state):
    gain_rows, shift_rows, w_qkv, w_attn, w_router, w_first, w_second = weights_all
    unit_one, factor_one, normed_one, qkv_rows, log_total, attended, unit_two, factor_two, normed_two, pick_table, gate_pair, cell_index, buffer_in, table_out = kept_state
    score_scale = HEAD_DIM ** (-0.5)
    row_count = IMGS * SEQ
    dump_cell = EXPERTS * N_EXPERT * CAP
    grad_flat = grad_rows.reshape(row_count, D)
    grad_wide = widen(grad_flat.astype(jnp.bfloat16))
    pieces = (gate_pair[..., None] * grad_wide[:, None, :]).astype(jnp.bfloat16).reshape(-1, D)
    buffer_grad = jnp.zeros((dump_cell + 1, D), jnp.bfloat16).at[cell_index.reshape(-1)].set(pieces)[:dump_cell].reshape(EXPERTS, N_EXPERT * CAP, D)
    grad_second, grad_first, input_part = lax.map(expert_back, (buffer_in, w_first, w_second, buffer_grad))
    table_in = jnp.concatenate([input_part.reshape(dump_cell, D), jnp.zeros((1, D), jnp.float32)], axis=0)
    routed = lax.optimization_barrier(jnp.sum(table_in[cell_index], axis=1))
    gate_grad = lax.optimization_barrier(jnp.sum(grad_wide[:, None, :] * table_out[cell_index], axis=-1))
    logit_grad = (gate_pair[:, 0] * gate_pair[:, 1] * (gate_grad[:, 0] - gate_grad[:, 1]))[:, None] * (pick_table[:, 0, :] - pick_table[:, 1, :])
    grad_router = jnp.dot(widen(normed_two).T, logit_grad, precision=highest)
    normed_grad = routed + jnp.dot(logit_grad, widen(w_router).T, precision=highest)
    mid_grad = grad_flat + norm_back(normed_grad, unit_two, factor_two, gain_rows[1])
    gain_two = lax.optimization_barrier(jnp.sum(normed_grad * unit_two, axis=0))
    shift_two = lax.optimization_barrier(jnp.sum(normed_grad, axis=0))
    mid_low = mid_grad.astype(jnp.bfloat16)
    grad_attn = jnp.dot(attended.T, mid_low, preferred_element_type=jnp.float32)
    attended_grad = widen(jnp.dot(mid_low, w_attn.reshape(D, D).T, preferred_element_type=jnp.float32).astype(jnp.bfloat16)).reshape(IMGS, SEQ, HEADS, HEAD_DIM)
    qkv_heads = widen(qkv_rows).reshape(3, IMGS, SEQ, HEADS, HEAD_DIM)
    scores = jnp.einsum('ishd,ithd->ihst', qkv_heads[0], qkv_heads[1]) * score_scale
    probs_wide = jnp.exp(scores - log_total)
    value_grad = jnp.einsum('ihst,ishd->ithd', widen(probs_wide.astype(jnp.bfloat16)), attended_grad).astype(jnp.bfloat16)
    prob_grad = jnp.einsum('ishd,ithd->ihst', attended_grad, qkv_heads[2])
    row_dot = lax.optimization_barrier(jnp.sum(probs_wide * prob_grad, axis=-1, keepdims=True))
    score_grad = widen((probs_wide * (prob_grad - row_dot) * score_scale).astype(jnp.bfloat16))
    query_grad = jnp.einsum('ihst,ithd->ishd', score_grad, qkv_heads[1]).astype(jnp.bfloat16)
    key_grad = jnp.einsum('ihst,ishd->ithd', score_grad, qkv_heads[0]).astype(jnp.bfloat16)
    qkv_grad = jnp.stack([query_grad, key_grad, value_grad]).reshape(3, row_count, D)
    grad_qkv = jnp.stack([jnp.dot(normed_one.T, qkv_grad[member], preferred_element_type=jnp.float32) for member in range(3)])
    first_grad = jnp.dot(qkv_grad[0], w_qkv[0].reshape(D, D).T, preferred_element_type=jnp.float32)
    first_grad = first_grad + jnp.dot(qkv_grad[1], w_qkv[1].reshape(D, D).T, preferred_element_type=jnp.float32)
    first_grad = first_grad + jnp.dot(qkv_grad[2], w_qkv[2].reshape(D, D).T, preferred_element_type=jnp.float32)
    start_grad = mid_grad + norm_back(first_grad, unit_one, factor_one, gain_rows[0])
    gain_one = lax.optimization_barrier(jnp.sum(first_grad * unit_one, axis=0))
    shift_one = lax.optimization_barrier(jnp.sum(first_grad, axis=0))
    grad_parts = (jnp.stack([gain_one, gain_two]), jnp.stack([shift_one, shift_two]), grad_qkv, grad_attn, grad_router, grad_first, grad_second)
    result = lax.optimization_barrier(start_grad.astype(jnp.bfloat16).reshape(grad_rows.shape))
    return (result, grad_parts)

def reference(tokens, cotangent, norm_gains, norm_shifts, w_qkv, w_attn_out, w_router, w_in, w_out, choices, slot_ranks):
    section_weights = [(norm_gains[level], norm_shifts[level], w_qkv[level], w_attn_out[level], w_router[level], w_in[level], w_out[level]) for level in range(2)]
    outputs_zero = []
    outputs_one = []
    grads_zero = []
    grads_one = []
    totals_zero = None
    totals_one = None
    for micro_index in range(MICRO):
        first_out, first_kept = layer_forward(tokens[micro_index], section_weights[0], choices[0, micro_index], slot_ranks[0, micro_index])
        second_out, second_kept = layer_forward(first_out, section_weights[1], choices[1, micro_index], slot_ranks[1, micro_index])
        second_grad, second_parts = layer_backward(cotangent[micro_index], section_weights[1], second_kept)
        first_grad, first_parts = layer_backward(widen(second_grad), section_weights[0], first_kept)
        outputs_zero.append(first_out)
        outputs_one.append(second_out)
        grads_zero.append(first_grad)
        grads_one.append(second_grad)
        totals_zero = first_parts if totals_zero is None else jax.tree.map(jnp.add, totals_zero, first_parts)
        totals_one = second_parts if totals_one is None else jax.tree.map(jnp.add, totals_one, second_parts)
    section_out = jnp.stack([jnp.stack(outputs_zero), jnp.stack(outputs_one)])
    input_grad = jnp.stack([jnp.stack(grads_zero), jnp.stack(grads_one)])
    merged = [jnp.stack([totals_zero[member], totals_one[member]]) for member in range(7)]
    return (section_out, input_grad, merged[0], merged[1], merged[2].reshape(2, 3, D, HEADS, HEAD_DIM), merged[3].reshape(2, HEADS, HEAD_DIM, D), merged[4], merged[5], merged[6])
```

```python
import jax
import jax.numpy as jnp
from jax import lax
from jax.sharding import PartitionSpec as P

HEAD_DIM = 64

norm_eps = 1e-06
half_root = 0.7071067811865476
tau_root = 0.3989422804014327
bf16 = jnp.bfloat16
f32 = jnp.float32


def gelu_value(values):
    return 0.5 * values * (1.0 + lax.erf(values * half_root))


def gelu_slope(values):
    return (
        0.5 * (1.0 + lax.erf(values * half_root))
        + values * jnp.exp(-0.5 * values * values) * tau_root
    )


def normalize(values, gain_row, shift_row):
    center = jnp.mean(values, axis=-1, keepdims=True)
    deviation = values - center
    factor = lax.rsqrt(jnp.mean(deviation * deviation, axis=-1, keepdims=True) + norm_eps)
    unit_rows = deviation * factor
    return (unit_rows * gain_row + shift_row, unit_rows, factor)


def norm_back(grad_norm, unit_rows, factor, gain_row):
    scaled = grad_norm * gain_row
    return factor * (
        scaled
        - jnp.mean(scaled, axis=-1, keepdims=True)
        - unit_rows * jnp.mean(scaled * unit_rows, axis=-1, keepdims=True)
    )


def dot(left, right):
    return jnp.dot(left, right, preferred_element_type=f32)


def dot_tn(left, right):
    return lax.dot_general(left, right, (((0,), (0,)), ((), ())), preferred_element_type=f32)


def dot_nt(left, right):
    return lax.dot_general(left, right, (((1,), (1,)), ((), ())), preferred_element_type=f32)


def flip(block, axis, mask):
    return lax.ppermute(block, axis, [(i, i ^ mask) for i in range(lax.axis_size(axis))])


def rotate(block, axis, distance):
    count = lax.axis_size(axis)
    return lax.ppermute(block, axis, [(i, (i + distance) % count) for i in range(count)])


def gather_rows(own):
    count = lax.axis_size("tensor")
    return jnp.concatenate([own] + [flip(own, "tensor", d) for d in range(1, count)], axis=0)


def sum_rows(terms):
    count = lax.axis_size("tensor")
    parts = terms.astype(bf16).reshape(count, -1, terms.shape[-1])
    arrived = [flip(parts[d], "tensor", d).astype(f32) for d in range(1, count)]
    total = parts[0].astype(f32)
    for part in arrived:
        total = total + part
    return total


def to_owners(blocks):
    count = lax.axis_size("expert")
    return jnp.stack([blocks[0]] + [rotate(blocks[d], "expert", d) for d in range(1, count)])


def from_owners(blocks):
    count = lax.axis_size("expert")
    return jnp.stack([blocks[0]] + [rotate(blocks[d], "expert", -d) for d in range(1, count)])


def route(picks, slots, capacity, local_count):
    count = lax.axis_size("expert")
    here = lax.axis_index("expert")
    owner = (picks // local_count - here) % count
    cell = (owner * local_count + picks % local_count) * capacity + slots
    return jnp.where(slots < capacity, cell, count * local_count * capacity)


def forward(rows_own, weights, picks, cells):
    gains, shifts, w_qkv, w_attn, w_router, w_first, w_second = weights
    length = picks.shape[0]
    features = rows_own.shape[-1]
    experts = w_router.shape[1]
    local_count = w_first.shape[0]
    owners = experts // local_count
    cell_count = CAPACITY(length, experts, owners) * experts
    heads = w_qkv.shape[1] // (3 * HEAD_DIM)
    start_own = rows_own.astype(f32)
    normed_one, unit_one, factor_one = normalize(start_own, gains[0], shifts[0])
    full_one = gather_rows(normed_one.astype(bf16))
    qkv = dot(full_one, w_qkv).astype(bf16)
    parts = qkv.reshape(length, 3, heads, HEAD_DIM)
    scores = jnp.einsum("shd,thd->hst", parts[:, 0], parts[:, 1], preferred_element_type=f32)
    scores = scores * HEAD_DIM ** (-0.5)
    log_total = jnp.log(jnp.sum(jnp.exp(scores), axis=-1, keepdims=True))
    soft = jnp.exp(scores - log_total).astype(bf16)
    attended = (
        jnp.einsum("hst,thd->shd", soft, parts[:, 2], preferred_element_type=f32)
        .astype(bf16)
        .reshape(length, -1)
    )
    middle_own = start_own + sum_rows(dot(attended, w_attn))
    normed_two, unit_two, factor_two = normalize(middle_own, gains[1], shifts[1])
    full_two = gather_rows(normed_two.astype(bf16))
    logits = dot(full_two, w_router)
    pick_table = (picks[..., None] == jnp.arange(experts)).astype(f32)
    chosen = jnp.sum(pick_table * logits[:, None, :], axis=-1)
    first_gate = jax.nn.sigmoid(chosen[:, 0] - chosen[:, 1])
    gates = jnp.stack([first_gate, 1.0 - first_gate], axis=-1)
    cell_ids = jnp.arange(cell_count)
    hit = cells.T[:, None, :] == cell_ids[None, :, None]
    select = (hit[0] | hit[1]).astype(bf16)
    cell_gates = jnp.sum(jnp.where(hit, gates.T[:, None, :], 0.0), axis=(0, 2))
    sending = dot(select, full_two).astype(bf16).reshape(owners, -1, features)
    arrived = to_owners(sending)
    arrived = arrived.reshape(owners, local_count, -1, features)
    inner = jnp.einsum("sjcd,jdf->jscf", arrived, w_first, preferred_element_type=f32)
    hidden = gelu_value(inner).astype(bf16)
    outer = jnp.einsum("jscf,jfd->sjcd", hidden, w_second, preferred_element_type=f32).astype(bf16)
    table = from_owners(outer.reshape(owners, -1, features)).reshape(cell_count, features)
    weighted = (select * cell_gates[:, None]).astype(bf16)
    mixed_own = sum_rows(dot_tn(weighted, table))
    result_own = (middle_own + mixed_own).astype(bf16)
    kept = (
        unit_one,
        factor_one,
        full_one,
        qkv,
        log_total,
        attended,
        unit_two,
        factor_two,
        full_two,
        pick_table,
        gates,
        select,
        cell_gates,
        arrived,
        inner,
        hidden,
        table,
    )
    return result_own, kept


def CAPACITY(length, experts, owners):
    return 2 * length // experts


def backward(grad_own, weights, cells, kept):
    gains, shifts, w_qkv, w_attn, w_router, w_first, w_second = weights
    (
        unit_one,
        factor_one,
        full_one,
        qkv,
        log_total,
        attended,
        unit_two,
        factor_two,
        full_two,
        pick_table,
        gates,
        select,
        cell_gates,
        arrived,
        inner,
        hidden,
        table,
    ) = kept
    length = full_one.shape[0]
    features = grad_own.shape[-1]
    local_count = w_first.shape[0]
    owners = w_router.shape[1] // local_count
    heads = w_qkv.shape[1] // (3 * HEAD_DIM)
    cell_count = select.shape[0]
    full_grad = gather_rows(grad_own.astype(bf16))
    picked = dot(select, full_grad)
    back_send = (picked * cell_gates[:, None]).astype(bf16)
    back = to_owners(back_send.reshape(owners, -1, features))
    back = back.reshape(owners, local_count, -1, features)
    hidden_grad = jnp.einsum("sjcd,jfd->jscf", back, w_second, preferred_element_type=f32)
    inner_grad = (hidden_grad * gelu_slope(inner)).astype(bf16)
    input_part = jnp.einsum(
        "jscf,jdf->sjcd", inner_grad, w_first, preferred_element_type=f32
    ).astype(bf16)
    input_back = from_owners(input_part.reshape(owners, -1, features)).reshape(cell_count, features)
    cell_grad = jnp.sum(picked * table.astype(f32), axis=-1)
    hit = cells[:, :, None] == jnp.arange(cell_count)
    gate_grad = jnp.sum(jnp.where(hit, cell_grad, 0.0), axis=-1)
    logit_grad = (gates[:, 0] * gates[:, 1] * (gate_grad[:, 0] - gate_grad[:, 1]))[:, None] * (
        pick_table[:, 0] - pick_table[:, 1]
    )
    logit_low = logit_grad.astype(bf16)
    grad_router = dot_tn(logit_low, full_two)
    normed_grad = sum_rows(dot_tn(select, input_back) + dot_nt(logit_low, w_router))
    mid_own = grad_own + norm_back(normed_grad, unit_two, factor_two, gains[1])
    gain_two = jnp.sum(normed_grad * unit_two, axis=0)
    shift_two = jnp.sum(normed_grad, axis=0)
    full_mid = gather_rows(mid_own.astype(bf16))
    attended_grad = dot_nt(full_mid, w_attn).astype(bf16).reshape(length, heads, HEAD_DIM)
    parts = qkv.reshape(length, 3, heads, HEAD_DIM)
    scores = jnp.einsum("shd,thd->hst", parts[:, 0], parts[:, 1], preferred_element_type=f32)
    probs = jnp.exp(scores * HEAD_DIM ** (-0.5) - log_total)
    value_grad = jnp.einsum(
        "hst,shd->thd", probs.astype(bf16), attended_grad, preferred_element_type=f32
    ).astype(bf16)
    prob_grad = jnp.einsum("shd,thd->hst", attended_grad, parts[:, 2], preferred_element_type=f32)
    row_dot = jnp.sum(probs * prob_grad, axis=-1, keepdims=True)
    score_grad = (probs * (prob_grad - row_dot) * HEAD_DIM ** (-0.5)).astype(bf16)
    query_grad = jnp.einsum(
        "hst,thd->shd", score_grad, parts[:, 1], preferred_element_type=f32
    ).astype(bf16)
    key_grad = jnp.einsum(
        "hst,shd->thd", score_grad, parts[:, 0], preferred_element_type=f32
    ).astype(bf16)
    qkv_grad = jnp.stack([query_grad, key_grad, value_grad], axis=1).reshape(length, -1)
    first_grad = sum_rows(dot_nt(qkv_grad, w_qkv))
    start_own = mid_own + norm_back(first_grad, unit_one, factor_one, gains[0])
    gain_one = jnp.sum(first_grad * unit_one, axis=0)
    shift_one = jnp.sum(first_grad, axis=0)
    small = jnp.concatenate(
        [jnp.stack([gain_one, gain_two, shift_one, shift_two]), grad_router], axis=0
    )
    dense = jnp.concatenate(
        [dot_tn(full_one, qkv_grad), dot_tn(full_mid, attended)], axis=1
    ).astype(bf16)
    return start_own.astype(bf16), small, dense, (back, inner_grad)


def reduce_over_images(block):
    count = lax.axis_size("expert")
    here = lax.axis_index("expert")
    parts = block.reshape(count, -1, block.shape[-1])
    total = lax.dynamic_index_in_dim(parts, here, 0, keepdims=False).astype(f32)
    arrived = [
        rotate(lax.dynamic_index_in_dim(parts, (here + d) % count, 0, keepdims=False), "expert", d)
        for d in range(1, count)
    ]
    for part in arrived:
        total = total + part.astype(f32)
    total = total.astype(bf16)
    held = jnp.concatenate([total] + [rotate(total, "expert", -d) for d in range(1, count)])
    return jnp.roll(held.reshape(parts.shape), here, axis=0).reshape(block.shape)


def per_device(
    tokens,
    cotangent,
    norm_gains,
    norm_shifts,
    w_qkv,
    w_attn_out,
    w_router,
    w_in,
    w_out,
    choices,
    slot_ranks,
):
    section = lax.axis_index("section")
    tensor = lax.axis_index("tensor")
    tensors = lax.axis_size("tensor")
    features = tokens.shape[3]
    own_rows = tokens.shape[2]
    length = choices.shape[3]
    experts = w_router.shape[2]
    local_count = w_in.shape[1]
    owners = experts // local_count
    capacity = CAPACITY(length, experts, owners)
    on_first = section == 0

    def swap(block):
        return flip(block, "section", 1)

    own_qkv = jnp.transpose(w_qkv[0], (1, 0, 2, 3)).reshape(features, -1)
    own_weights = (
        norm_gains[0],
        norm_shifts[0],
        own_qkv,
        w_attn_out[0].reshape(-1, features),
        w_router[0],
        w_in[0],
        w_out[0],
    )
    their_weights = tuple(swap(weight) for weight in own_weights)
    layer_weights = [
        tuple(
            jnp.where(section == layer, own, their)
            for own, their in zip(own_weights, their_weights)
        )
        for layer in range(2)
    ]
    order = jnp.arange(tensors) ^ tensor
    table = jnp.stack([choices[0, :, 0], slot_ranks[0, :, 0]], axis=1)
    table = table.reshape(2, 2, tensors, own_rows, 2)[:, :, order].reshape(2, 2, length, 2)
    mine = jnp.where(on_first, table[0], table[1])
    theirs = swap(jnp.where(on_first, table[1], table[0]))
    routes = [
        jnp.where(section == layer, mine, theirs)
        for layer in range(2)
    ]
    picks = [r[0] for r in routes]
    cells = [route(r[0], r[1], capacity, local_count) for r in routes]

    rows = jnp.where(on_first, tokens[0, 0], tokens[1, 0])
    results, kept_all = [], []
    for layer in range(2):
        rows, kept = forward(rows, layer_weights[layer], picks[layer], cells[layer])
        results.append(rows)
        kept_all.append(kept)

    def to_layer_owner(first_layer, second_layer):
        mine = jnp.where(on_first, first_layer, second_layer)
        theirs = swap(jnp.where(on_first, second_layer, first_layer))
        return mine, theirs

    def by_micro(first_layer, second_layer):
        mine, theirs = to_layer_owner(first_layer, second_layer)
        return jnp.stack(
            [jnp.where(on_first, mine, theirs), jnp.where(on_first, theirs, mine)]
        )

    section_out = by_micro(*results)[None, :, None]
    grad = jnp.where(on_first, cotangent[0, 0], cotangent[1, 0])
    grads = [None, None]
    smalls = [None, None]
    denses = [None, None]
    sides = [None, None]
    for layer in (1, 0):
        low, smalls[layer], denses[layer], sides[layer] = backward(
            grad, layer_weights[layer], cells[layer], kept_all[layer]
        )
        grads[layer] = low
        grad = low.astype(f32)
    input_grad = by_micro(*grads)[None, :, None]

    def pair_sum(first_layer, second_layer):
        mine, theirs = to_layer_owner(first_layer, second_layer)
        return mine.astype(f32) + theirs.astype(f32)

    small = pair_sum(*smalls)
    for d in (1, 2):
        small = small + flip(small, "tensor", d)
    step = 1
    while step < lax.axis_size("expert"):
        small = small + flip(small, "expert", step)
        step *= 2
    dense = reduce_over_images(pair_sum(*denses).astype(bf16)).astype(f32)
    qkv_width = own_qkv.shape[1]
    qkv_total = jnp.transpose(
        dense[:, :qkv_width].reshape(features, 3, -1, HEAD_DIM), (1, 0, 2, 3)
    )
    attn_total = dense[:, qkv_width:].T

    def expert_rows(value):
        return jnp.swapaxes(value, 0, 1)

    def weight_grad(lefts, rights):
        left_own, left_their = to_layer_owner(*lefts)
        right_own, right_their = to_layer_owner(*rights)
        return jnp.einsum(
            "jscd,jscf->jdf", left_own, right_own, preferred_element_type=f32
        ) + jnp.einsum("jscd,jscf->jdf", left_their, right_their, preferred_element_type=f32)

    arrived = [expert_rows(kept[13]) for kept in kept_all]
    hidden = [kept[15] for kept in kept_all]
    back = [expert_rows(side[0]) for side in sides]
    inner_grad = [side[1] for side in sides]
    grad_first = weight_grad(arrived, inner_grad)
    grad_second = weight_grad(hidden, back)
    return (
        section_out,
        input_grad,
        small[0:2][None],
        small[2:4][None],
        qkv_total.reshape(w_qkv.shape),
        attn_total.reshape(w_attn_out.shape),
        small[4:].T[None],
        grad_first[None],
        grad_second[None],
    )


def solution(mesh):
    return jax.shard_map(
        per_device,
        mesh=mesh,
        in_specs=(
            P(None, "expert", "tensor", None),
            P(None, "expert", "tensor", None),
            P("section", None, None),
            P("section", None, None),
            P("section", None, None, "tensor", None),
            P("section", "tensor", None, None),
            P("section", None, None),
            P("section", "expert", None, "tensor"),
            P("section", "expert", "tensor", None),
            P("section", None, "expert", None, None),
            P("section", None, "expert", None, None),
        ),
        out_specs=(
            P("section", None, "expert", "tensor", None),
            P("section", None, "expert", "tensor", None),
            P("section", None, None),
            P("section", None, None),
            P("section", None, None, "tensor", None),
            P("section", "tensor", None, None),
            P("section", None, None),
            P("section", "expert", None, "tensor"),
            P("section", "expert", "tensor", None),
        ),
        check_vma=False,
    )
```

```python
import functools

import jax
import jax.numpy as jnp
from jax import lax
from jax.experimental import pallas as pl
from jax.experimental.pallas import tpu as pltpu
from jax.sharding import PartitionSpec as P

HEAD_DIM = 64

norm_eps = 1e-06
half_root = 0.7071067811865476
tau_root = 0.3989422804014327
bf16 = jnp.bfloat16
f32 = jnp.float32


def gelu_value(values):
    return 0.5 * values * (1.0 + lax.erf(values * half_root))


def gelu_slope(values):
    return (
        0.5 * (1.0 + lax.erf(values * half_root))
        + values * jnp.exp(-0.5 * values * values) * tau_root
    )


def unit_of(values):
    center = jnp.mean(values, axis=-1, keepdims=True)
    deviation = values - center
    factor = lax.rsqrt(jnp.mean(deviation * deviation, axis=-1, keepdims=True) + norm_eps)
    return deviation * factor, factor


def norm_back(grad_norm, unit_rows, factor, gain_row):
    scaled = grad_norm * gain_row
    return factor * (
        scaled
        - jnp.mean(scaled, axis=-1, keepdims=True)
        - unit_rows * jnp.mean(scaled * unit_rows, axis=-1, keepdims=True)
    )


def dot(left, right):
    return jnp.dot(left, right, preferred_element_type=f32)


def dot_tn(left, right):
    return lax.dot_general(left, right, (((0,), (0,)), ((), ())), preferred_element_type=f32)


def dot_nt(left, right):
    return lax.dot_general(left, right, (((1,), (1,)), ((), ())), preferred_element_type=f32)


def flip(block, axis, mask):
    return lax.ppermute(block, axis, [(i, i ^ mask) for i in range(lax.axis_size(axis))])


def rotate(block, axis, distance):
    count = lax.axis_size(axis)
    return lax.ppermute(block, axis, [(i, (i + distance) % count) for i in range(count)])


def gather_tensor(own):
    return [own] + [flip(own, "tensor", d) for d in range(1, lax.axis_size("tensor"))]


def exchange_tensor(parts):
    return [parts[0]] + [flip(parts[d], "tensor", d) for d in range(1, len(parts))]


def to_owners(blocks):
    return [blocks[0]] + [rotate(blocks[d], "expert", d) for d in range(1, len(blocks))]


def from_owners(blocks):
    return [blocks[0]] + [rotate(blocks[d], "expert", -d) for d in range(1, len(blocks))]


def joined_rows(refs):
    return jnp.concatenate([ref[...] for ref in refs], axis=0)


def lane_mask(head, width):
    lanes = lax.broadcasted_iota(jnp.int32, (1, width), 1)
    return (lanes // HEAD_DIM == head).astype(bf16)


def pick_rows(cell_column, count):
    ids = lax.broadcasted_iota(jnp.int32, (cell_column.shape[0], count), 1)
    return ids == cell_column


def pick_cells(cell_row, count):
    ids = lax.broadcasted_iota(jnp.int32, (count, cell_row.shape[1]), 0)
    return ids == cell_row


def expert_sign(pick_column, experts):
    ids = lax.broadcasted_iota(jnp.int32, (pick_column.shape[0], experts), 1)
    return (ids == pick_column).astype(f32)


def combine(middle, gate, cells, table):
    count = table.shape[0]
    first = dot(pick_rows(cells[:, 0:1], count).astype(bf16), table)
    second = dot(pick_rows(cells[:, 1:2], count).astype(bf16), table)
    return middle + gate * first + (1.0 - gate) * second, first - second


def combine_kernel(middle_ref, gate_ref, cells_ref, *refs):
    result_ref, gap_ref = refs[-2:]
    total, gap = combine(
        middle_ref[...], gate_ref[:, 0:1], cells_ref[...], joined_rows(refs[:-2])
    )
    result_ref[...] = total.astype(bf16)
    gap_ref[...] = gap.astype(bf16)


class Weights:
    def __init__(self, layer, flag_ref, refs, held_ref, sems, blocks):
        own, swapped = refs[:2]
        pieces = (len(refs) - 2) // 2
        mine, theirs = refs[2 : 2 + pieces], refs[2 + pieces :]
        width = held_ref.shape[1] // 4
        self.held, self.sems, self.width = held_ref, sems, width
        self.own, self.piece = own, mine[0]
        self.first = blocks[0]
        on_first = flag_ref[0] == 0
        here = flag_ref[0] == layer

        def fetch(source, block, begin, size, sem):
            place = held_ref.at[block - self.first, pl.ds(begin, size)]
            pltpu.make_async_copy(source, place, sems.at[sem]).start()

        def fetch_all(low, high):
            for block in blocks:
                for k in range(2 if block else 0):
                    index = 2 * (block - 1) + k
                    fetch(low[index], block, k * width, width, 4 * (block - 1) + k + 1)
                    fetch(high[index], block, (k + 2) * width, width, 4 * (block - 1) + k + 3)

        if 0 in blocks:

            @pl.when(here)
            def _():
                fetch(own, 0, 0, 4 * width, 0)

            @pl.when(jnp.logical_not(here))
            def _():
                fetch(swapped, 0, 0, 4 * width, 0)

        @pl.when(on_first)
        def _():
            fetch_all(mine, theirs)

        @pl.when(jnp.logical_not(on_first))
        def _():
            fetch_all(theirs, mine)

    def wait(self, block):
        width = self.width
        if block == 0:
            pltpu.make_async_copy(self.own, self.held.at[0], self.sems.at[0]).wait()
            return
        for k in range(4):
            place = self.held.at[block - self.first, pl.ds(k * width, width)]
            pltpu.make_async_copy(self.piece, place, self.sems.at[4 * (block - 1) + 1 + k]).wait()

    def member(self, block, index):
        return self.held[block - self.first, pl.ds(index * self.width, self.width)]


def front_kernel(layer, joined, tensors, weight_count, *refs):
    refs = list(refs)
    flag_ref = refs.pop(0)
    if joined:
        before_ref, before_gate_ref, before_cells_ref = refs[:3]
        refs = refs[3:]
    table_refs, refs = refs[:tensors], refs[tensors:]
    norms_ref, router_ref, picks_ref, cells_ref = refs[:4]
    weight_refs, refs = refs[4 : 4 + weight_count], refs[4 + weight_count :]
    if joined:
        result_ref, gap_ref = refs[:2]
        refs = refs[2:]
    normed_ref, heads_ref, middle_ref, second_ref, gate_ref, send_ref, held_ref, sems = refs
    weights = Weights(layer, flag_ref, weight_refs, held_ref, sems, range(tensors))
    if joined:
        total, gap = combine(
            before_ref[...], before_gate_ref[:, 0:1], before_cells_ref[...], joined_rows(table_refs)
        )
        low = total.astype(bf16)
        result_ref[...] = low
        gap_ref[...] = gap.astype(bf16)
    else:
        low = joined_rows(table_refs)
    start = low.astype(f32)
    unit, _ = unit_of(start)
    normed_ref[...] = (unit * norms_ref[0:1] + norms_ref[2:3]).astype(bf16)
    middle_ref[...] = start
    for block in range(tensors):
        weights.wait(block)
        normed = normed_ref[...]
        query = dot_nt(normed, weights.member(block, 0)).astype(bf16)
        key = dot_nt(normed, weights.member(block, 1)).astype(bf16)
        value = dot_nt(normed, weights.member(block, 2)).astype(bf16)
        width = query.shape[1]
        attended = jnp.zeros(query.shape, f32)
        for head in range(width // HEAD_DIM):
            mask = lane_mask(head, width)
            scores = dot_nt(query * mask, key) * HEAD_DIM ** (-0.5)
            raised = jnp.exp(scores)
            soft = raised * (1.0 / jnp.sum(raised, axis=-1, keepdims=True))
            attended = attended + dot(soft.astype(bf16), value * mask)
        attended = attended.astype(bf16)
        heads_ref[block, 0] = query
        heads_ref[block, 1] = key
        heads_ref[block, 2] = value
        heads_ref[block, 3] = attended
        middle_ref[...] += dot(attended, weights.member(block, 3))
    unit, _ = unit_of(middle_ref[...])
    second = (unit * norms_ref[1:2] + norms_ref[3:4]).astype(bf16)
    second_ref[...] = second
    logits = dot_nt(second, router_ref[...])
    experts = logits.shape[1]
    sign = expert_sign(picks_ref[:, 0:1], experts) - expert_sign(picks_ref[:, 1:2], experts)
    gap = jnp.sum(sign * logits, axis=-1, keepdims=True)
    gate = 1.0 / (1.0 + jnp.exp(-gap))
    gate_ref[...] = jnp.broadcast_to(gate, gate_ref.shape)
    count = send_ref.shape[0]
    hit = pick_cells(cells_ref[0:1], count) | pick_cells(cells_ref[1:2], count)
    send_ref[...] = dot(hit.astype(bf16), second).astype(bf16)


def spread(grad, gate, cells_row, count):
    wide = grad.astype(f32)
    first = (wide * gate).astype(bf16)
    second = (wide * (1.0 - gate)).astype(bf16)
    total = dot(pick_cells(cells_row[0:1], count).astype(bf16), first)
    total = total + dot(pick_cells(cells_row[1:2], count).astype(bf16), second)
    return total.astype(bf16)


def spread_kernel(gate_ref, cells_ref, *refs):
    grad_refs, (grad_ref, send_ref) = refs[:-2], refs[-2:]
    grad = joined_rows(grad_refs)
    grad_ref[...] = grad
    send_ref[...] = spread(grad, gate_ref[:, 0:1], cells_ref[...], send_ref.shape[0])


def back_heads(weights, block, low, heads_ref, total_ref):
    weights.wait(block)
    out_grad = dot_nt(low, weights.member(block, 3)).astype(bf16)
    query = heads_ref[block, 0]
    key = heads_ref[block, 1]
    value = heads_ref[block, 2]
    width = query.shape[1]
    query_grad = jnp.zeros(query.shape, f32)
    key_grad = jnp.zeros(query.shape, f32)
    value_grad = jnp.zeros(query.shape, f32)
    for head in range(width // HEAD_DIM):
        mask = lane_mask(head, width)
        own_key = key * mask
        raised = jnp.exp(dot_nt(own_key, query) * HEAD_DIM ** (-0.5))
        probs = raised * (1.0 / jnp.sum(raised, axis=0, keepdims=True))
        prob_grad = dot_nt(value * mask, out_grad)
        row_dot = jnp.sum(probs * prob_grad, axis=0, keepdims=True)
        score_grad = (probs * (prob_grad - row_dot) * HEAD_DIM ** (-0.5)).astype(bf16)
        value_grad = value_grad + dot(probs.astype(bf16), out_grad * mask)
        key_grad = key_grad + dot(score_grad, query * mask)
        query_grad = query_grad + dot_tn(score_grad, own_key)
    made = (query_grad.astype(bf16), key_grad.astype(bf16), value_grad.astype(bf16))
    part = dot(made[0], weights.member(block, 0))
    part = part + dot(made[1], weights.member(block, 1)) + dot(made[2], weights.member(block, 2))
    if block == 0:
        total_ref[...] = part
    else:
        total_ref[...] += part
    return made


def back_first_kernel(layer, tensors, weight_count, *refs):
    refs = list(refs)
    (
        flag_ref,
        grad_ref,
        gap_ref,
        gate_ref,
        picks_ref,
        cells_ref,
        router_ref,
        norms_ref,
        middle_ref,
        second_ref,
        heads_ref,
    ) = refs[:11]
    refs = refs[11:]
    table_refs, refs = refs[:tensors], refs[tensors:]
    weight_refs, refs = refs[:weight_count], refs[weight_count:]
    own_ref, low_ref, small_ref, mid_ref, total_ref, held_ref, sems = refs
    experts = router_ref.shape[0]
    weights = Weights(layer, flag_ref, weight_refs, held_ref, sems, [0])
    grad = grad_ref[...].astype(f32)
    gate = gate_ref[:, 0:1]
    change = jnp.sum(grad * gap_ref[...].astype(f32), axis=-1, keepdims=True)
    sign = expert_sign(picks_ref[:, 0:1], experts) - expert_sign(picks_ref[:, 1:2], experts)
    logit_grad = (gate * (1.0 - gate) * change * sign).astype(bf16)
    table = joined_rows(table_refs)
    count = table.shape[0]
    hit = pick_rows(cells_ref[:, 0:1], count) | pick_rows(cells_ref[:, 1:2], count)
    normed_grad = dot(hit.astype(bf16), table) + dot(logit_grad, router_ref[...])
    unit, factor = unit_of(middle_ref[...])
    mid = grad + norm_back(normed_grad, unit, factor, norms_ref[1:2])
    small_ref[...] = jnp.zeros_like(small_ref)
    small_ref[1:2] = jnp.sum(normed_grad * unit, axis=0, keepdims=True)
    small_ref[3:4] = jnp.sum(normed_grad, axis=0, keepdims=True)
    small_ref[8 : 8 + experts] = dot_tn(logit_grad, second_ref[...])
    mid_ref[...] = mid
    low = mid.astype(bf16)
    low_ref[...] = low
    made = back_heads(weights, 0, low, heads_ref, total_ref)
    for index in range(3):
        own_ref[index] = made[index]


def back_rest_kernel(layer, chained, tensors, weight_count, *refs):
    refs = list(refs)
    flag_ref, low_ref, mid_ref, before_ref, norms_ref, start_ref, heads_ref = refs[:7]
    refs = refs[7:]
    weight_refs, refs = refs[:weight_count], refs[weight_count:]
    if chained:
        next_gate_ref, next_cells_ref = refs[:2]
        refs = refs[2:]
    out_ref, small_ref = refs[:2]
    refs = refs[2:]
    if chained:
        send_ref = refs.pop(0)
    total_ref, held_ref, sems = refs
    weights = Weights(layer, flag_ref, weight_refs, held_ref, sems, range(1, tensors))
    total_ref[...] = before_ref[...]
    for block in range(1, tensors):
        back_heads(weights, block, low_ref[...], heads_ref, total_ref)
    first_grad = total_ref[...]
    unit, factor = unit_of(start_ref[...].astype(f32))
    small_ref[...] = jnp.zeros_like(small_ref)
    small_ref[0:1] = jnp.sum(first_grad * unit, axis=0, keepdims=True)
    small_ref[2:3] = jnp.sum(first_grad, axis=0, keepdims=True)
    result = (mid_ref[...] + norm_back(first_grad, unit, factor, norms_ref[0:1])).astype(bf16)
    out_ref[...] = result
    if chained:
        send_ref[...] = spread(
            result, next_gate_ref[:, 0:1], next_cells_ref[...], send_ref.shape[0]
        )


def with_either(chosen, own_refs, their_refs, body):
    @pl.when(chosen)
    def _():
        body(*own_refs)

    @pl.when(jnp.logical_not(chosen))
    def _():
        body(*their_refs)


def expert_kernel(layer, tensors, flag_ref, *refs):
    row_refs, refs = refs[:tensors], refs[tensors:]
    own_refs, their_refs, refs = refs[:2], refs[2:4], refs[4:]
    out_refs, (packed_ref, hidden_ref, slope_ref) = refs[:tensors], refs[tensors:]

    def body(first_ref, second_ref):
        rows = jnp.concatenate([ref[0] for ref in row_refs], axis=0)
        packed_ref[0] = rows
        inner = dot(rows, first_ref[0])
        hidden = gelu_value(inner).astype(bf16)
        hidden_ref[0] = hidden
        slope_ref[0] = gelu_slope(inner).astype(bf16)
        outer = dot(hidden, second_ref[0]).astype(bf16)
        size = outer.shape[0] // tensors
        for d in range(tensors):
            out_refs[d][0] = outer[d * size : (d + 1) * size]

    with_either(flag_ref[0] == layer, own_refs, their_refs, body)


def expert_back_kernel(layer, tensors, flag_ref, *refs):
    row_refs, refs = refs[:tensors], refs[tensors:]
    slope_ref = refs[0]
    own_refs, their_refs, refs = refs[1:3], refs[3:5], refs[5:]
    out_refs, (packed_ref, inner_ref) = refs[:tensors], refs[tensors:]

    def body(first_ref, second_ref):
        rows = jnp.concatenate([ref[0] for ref in row_refs], axis=0)
        packed_ref[0] = rows
        inner_grad = (dot_nt(rows, second_ref[0]) * slope_ref[0].astype(f32)).astype(bf16)
        inner_ref[0] = inner_grad
        outer = dot_nt(inner_grad, first_ref[0]).astype(bf16)
        size = outer.shape[0] // tensors
        for d in range(tensors):
            out_refs[d][0] = outer[d * size : (d + 1) * size]

    with_either(flag_ref[0] == layer, own_refs, their_refs, body)


def shaped(shape, dtype):
    return jax.ShapeDtypeStruct(shape, dtype)


def cost_of(flops, byte_count):
    return pl.CostEstimate(flops=flops, bytes_accessed=byte_count, transcendentals=0)


LIMIT = 48 * 1024 * 1024
IN_VMEM = pl.BlockSpec(memory_space=pltpu.VMEM)
IN_SMEM = pl.BlockSpec(memory_space=pltpu.SMEM)
ANYWHERE = pl.BlockSpec(memory_space=pl.ANY)


def run_kernel(kernel, args, kinds, outs, scratch=(), cost=None):
    return pl.pallas_call(
        kernel,
        in_specs=[kinds.get(i, IN_VMEM) for i in range(len(args))],
        out_specs=[IN_VMEM] * len(outs),
        out_shape=outs,
        scratch_shapes=list(scratch),
        cost_estimate=cost,
        compiler_params=pltpu.CompilerParams(vmem_limit_bytes=LIMIT),
    )(*args)


def weight_scratch(weights, blocks, tensors):
    rows, features = weights[0].shape
    return [
        pltpu.VMEM((blocks, rows, features), bf16),
        pltpu.SemaphoreType.DMA((4 * tensors - 3,)),
    ]


def front(layer, flag, start, tables, norms, router, picks, cells_row, weights, share):
    joined = start is not None
    tensors = len(tables)
    length = picks.shape[0]
    rows, features = weights[0].shape
    rows_low = shaped((length, features), bf16)
    outs = [rows_low, rows_low] if joined else []
    outs = outs + [
        rows_low,
        shaped((tensors, 4, length, rows // 4), bf16),
        shaped((length, features), f32),
        rows_low,
        shaped((length, 128), f32),
        shaped((share, features), bf16),
    ]
    args = [flag] + list(start or ()) + list(tables) + [norms, router, picks, cells_row]
    kinds = {0: IN_SMEM}
    kinds.update({len(args) + i: ANYWHERE for i in range(len(weights))})
    return run_kernel(
        functools.partial(front_kernel, layer, joined, tensors, len(weights)),
        args + list(weights),
        kinds,
        outs,
        weight_scratch(weights, tensors, tensors),
        cost_of(3_000_000_000, 9_000_000),
    )


def join(middle, gate, cells, tables):
    rows_low = shaped(middle.shape, bf16)
    return run_kernel(
        combine_kernel, [middle, gate, cells] + list(tables), {}, [rows_low, rows_low],
        cost=cost_of(800_000_000, 3_000_000),
    )


def spread_rows(gate, cells_row, grads, share):
    length = gate.shape[0]
    features = grads[0].shape[1]
    outs = [shaped((length, features), bf16), shaped((share, features), bf16)]
    return run_kernel(
        spread_kernel, [gate, cells_row] + list(grads), {}, outs, cost=cost_of(100_000_000, 1_000_000)
    )


def back_first(layer, flag, grad, gap, gate, picks, cells, router, norms, middle, second, heads, tables, weights):
    length, features = grad.shape
    tensors = len(tables)
    width = heads.shape[3]
    experts = router.shape[0]
    args = [flag, grad, gap, gate, picks, cells, router, norms, middle, second, heads] + list(tables)
    kinds = {0: IN_SMEM}
    kinds.update({len(args) + i: ANYWHERE for i in range(len(weights))})
    wide = shaped((length, features), f32)
    outs = [
        shaped((3, length, width), bf16),
        shaped((length, features), bf16),
        shaped((8 + experts, features), f32),
        wide,
        wide,
    ]
    return run_kernel(
        functools.partial(back_first_kernel, layer, tensors, len(weights)),
        args + list(weights),
        kinds,
        outs,
        weight_scratch(weights, 1, tensors),
        cost_of(2_000_000_000, 6_000_000),
    )


def back_rest(layer, flag, low, mid, total, norms, start, heads, weights, following):
    length, features = low.shape
    tensors = heads.shape[0]
    args = [flag, low, mid, total, norms, start, heads]
    kinds = {0: IN_SMEM}
    kinds.update({len(args) + i: ANYWHERE for i in range(len(weights))})
    args = args + list(weights)
    outs = [shaped((length, features), bf16), shaped((8, features), f32)]
    chained = following is not None
    if chained:
        next_gate, next_cells, share = following
        args = args + [next_gate, next_cells]
        outs = outs + [shaped((share, features), bf16)]
    return run_kernel(
        functools.partial(back_rest_kernel, layer, chained, tensors, len(weights)),
        args,
        kinds,
        outs,
        [pltpu.VMEM((length, features), f32)] + weight_scratch(weights, tensors - 1, tensors),
        cost_of(4_000_000_000, 9_000_000),
    )


def run_experts(kernel, layer, flag, rows, more, own, theirs, extra):
    local, size, features = rows[0].shape
    tensors = len(rows)

    def block(shape):
        return pl.BlockSpec((1,) + tuple(shape[1:]), lambda j, flag_ref: (j, 0, 0))

    def weight(shape, wanted):
        def index(j, flag_ref):
            return (jnp.where((flag_ref[0] == layer) == wanted, j, 0), 0, 0)

        return pl.BlockSpec((1,) + tuple(shape[1:]), index)

    args = list(rows) + list(more)
    specs = [block(a.shape) for a in args]
    specs = specs + [weight(w.shape, True) for w in own] + [weight(w.shape, False) for w in theirs]
    outs = [shaped(r.shape, bf16) for r in rows] + list(extra)
    return pl.pallas_call(
        functools.partial(kernel, layer, tensors),
        grid_spec=pltpu.PrefetchScalarGridSpec(
            num_scalar_prefetch=1,
            grid=(local,),
            in_specs=specs,
            out_specs=[block(o.shape) for o in outs],
        ),
        out_shape=outs,
        cost_estimate=cost_of(1_200_000_000, 9_000_000),
        compiler_params=pltpu.CompilerParams(
            dimension_semantics=("arbitrary",), vmem_limit_bytes=LIMIT
        ),
    )(flag, *args, *own, *theirs)


def per_device(
    tokens,
    cotangent,
    norm_gains,
    norm_shifts,
    w_qkv,
    w_attn_out,
    w_router,
    w_in,
    w_out,
    choices,
    slot_ranks,
):
    section = lax.axis_index("section")
    tensor = lax.axis_index("tensor")
    here = lax.axis_index("expert")
    tensors = lax.axis_size("tensor")
    owners = lax.axis_size("expert")
    features = tokens.shape[3]
    own_rows = tokens.shape[2]
    length = choices.shape[3]
    experts = w_router.shape[2]
    local = w_in.shape[1]
    hidden_count = w_in.shape[3]
    capacity = 2 * length // experts
    part = capacity // tensors
    share = experts * part
    on_first = section == 0
    flag = section.astype(jnp.int32).reshape(1)

    def swap(block):
        return flip(block, "section", 1)

    def both_layers(block):
        theirs = swap(block)
        return [jnp.where(section == layer, block, theirs) for layer in range(2)]

    def by_core(first, second):
        return jnp.where(on_first, first, second)

    own_weight = jnp.concatenate(
        [
            jnp.transpose(w_qkv[0], (0, 2, 3, 1)).reshape(-1, features),
            w_attn_out[0].reshape(-1, features),
        ]
    )
    swapped_weight = swap(own_weight)
    half = own_weight.shape[0] // 2

    def all_heads(layer):
        if layer == 0:
            piece = by_core(own_weight[:half], swapped_weight[half:])
        else:
            piece = by_core(swapped_weight[:half], own_weight[half:])
        one, two = piece[: half // 2], piece[half // 2 :]
        with jax.named_scope("near%d" % layer):
            one_x, two_y = flip(one, "tensor", 1), flip(two, "tensor", 2)
        with jax.named_scope("side%d" % layer):
            one_y, two_x = flip(one, "tensor", 2), flip(two, "tensor", 1)
        with jax.named_scope("far%d" % layer):
            one_far, two_far = flip(one_x, "tensor", 2), flip(two_y, "tensor", 1)
        mine = [one_x, two_x, one_y, two_y, one_far, two_far]
        return [own_weight, swapped_weight] + mine + [swap(block) for block in mine]

    weights = [all_heads(0), None]
    rows = gather_tensor(by_core(tokens[0, 0], tokens[1, 0]))

    order = jnp.arange(tensors) ^ tensor
    table = jnp.stack([choices[0, :, 0], slot_ranks[0, :, 0]], axis=1)
    table = jnp.swapaxes(table, 2, 3)
    mine = by_core(table[0], table[1])
    theirs = swap(by_core(table[1], table[0]))
    picks, cells, cells_row = [], [], []
    for layer in range(2):
        route = jnp.where(section == layer, mine, theirs)
        route = route.reshape(2, 2, tensors, own_rows)[:, :, order].reshape(2, 2, length)
        pick, slot = route[0], route[1]
        owner = (pick // local - here) % owners
        block = (slot // part) ^ tensor
        cell = block * share + (owner * local + pick % local) * part + slot % part
        cell = jnp.where(slot < capacity, cell, tensors * share)
        picks.append(pick.T)
        cells.append(cell.T)
        cells_row.append(cell)

    norms = both_layers(jnp.concatenate([norm_gains[0], norm_shifts[0]]))
    router = both_layers(w_router[0].T)
    own_experts = (w_in[0], w_out[0])
    their_experts = (swap(w_in[0]), swap(w_out[0]))

    def send_out(sent):
        arrived = to_owners(list(sent.reshape(owners, local, part, features)))
        return gather_tensor(jnp.concatenate(arrived, axis=1))

    def bring_back(parts):
        came = exchange_tensor(parts)
        total = came[0].astype(f32)
        for one in came[1:]:
            total = total + one.astype(f32)
        total = total.astype(bf16)
        blocks = [total[:, s * part : (s + 1) * part].reshape(-1, features) for s in range(owners)]
        return gather_tensor(jnp.concatenate(from_owners(blocks)))

    packed = shaped((local, tensors * owners * part, features), bf16)
    packed_hidden = shaped((local, tensors * owners * part, hidden_count), bf16)
    kept = []
    start, tables = None, rows
    for layer in range(2):
        made = front(
            layer, flag, start, tables, norms[layer], router[layer], picks[layer], cells_row[layer],
            weights[layer], share,
        )
        if layer:
            kept[0]["result"], kept[0]["gap"] = made[:2]
            base = made[0]
            made = made[2:]
        else:
            base = jnp.concatenate(rows)
            weights[1] = all_heads(1)
        normed, heads, middle, second, gate, sent = made
        arrived = send_out(sent)
        done = run_experts(
            expert_kernel, layer, flag, arrived, (), own_experts, their_experts,
            (packed, packed_hidden, packed_hidden),
        )
        tables = bring_back(done[:tensors])
        start = (middle, gate, cells[layer])
        kept.append(
            dict(
                rows=base, normed=normed, heads=heads, middle=middle, second=second, gate=gate,
                arrived=done[tensors], hidden=done[tensors + 1], slope=done[tensors + 2],
            )
        )
    kept[1]["result"], kept[1]["gap"] = join(*start, tables)

    def to_layer_owner(first_layer, second_layer):
        return by_core(first_layer, second_layer), swap(by_core(second_layer, first_layer))

    def by_micro(first_layer, second_layer):
        mine, theirs = to_layer_owner(first_layer, second_layer)
        return jnp.stack([by_core(mine, theirs), by_core(theirs, mine)])

    section_out = by_micro(kept[0]["result"][:own_rows], kept[1]["result"][:own_rows])

    def images_begin(block):
        size = block.shape[0] // 2
        mine = by_core(block[:size], block[size:])
        theirs = swap(by_core(block[size:], block[:size]))
        total = (mine.astype(f32) + theirs.astype(f32)).astype(bf16)
        return total.reshape(owners, -1, features)

    def images_sum(parts):
        total = lax.dynamic_index_in_dim(parts, here, 0, keepdims=False).astype(f32)
        for d in range(1, owners):
            piece = lax.dynamic_index_in_dim(parts, (here + d) % owners, 0, keepdims=False)
            total = total + rotate(piece, "expert", d).astype(f32)
        return total.astype(bf16)

    def images_end(total):
        held = jnp.stack([total] + [rotate(total, "expert", -d) for d in range(1, owners)])
        return jnp.roll(held, here, axis=0).reshape(-1, features)

    def sum_small(small):
        small = small + swap(small)
        step = 1
        while step < owners:
            small = small + flip(small, "expert", step)
            step *= 2
        return small

    def dense_of(kept_layer, own_grad, low):
        pieces = [dot_tn(own_grad[member], kept_layer["normed"]) for member in range(3)]
        pieces.append(dot_tn(kept_layer["heads"][0, 3], low))
        return jnp.concatenate([piece.astype(bf16) for piece in pieces])

    gathered = gather_tensor(by_core(cotangent[0, 0], cotangent[1, 0]).astype(bf16))
    grad, sent = spread_rows(kept[1]["gate"], cells_row[1], gathered, share)
    grads, smalls, denses, backs, inner_grads = [None] * 2, [None] * 2, [None] * 2, [None] * 2, [None] * 2
    for layer in (1, 0):
        k = kept[layer]
        came = send_out(sent)
        done = run_experts(
            expert_back_kernel, layer, flag, came, (k["slope"],), own_experts, their_experts,
            (packed, packed_hidden),
        )
        backs[layer], inner_grads[layer] = done[tensors:]
        tables = bring_back(done[:tensors])
        if layer == 0:
            tables, denses[1] = lax.optimization_barrier((tables, denses[1]))
        following = (kept[0]["gate"], cells_row[0], share) if layer else None
        own_grad, low, small, mid, total = back_first(
            layer, flag, grad, k["gap"], k["gate"], picks[layer], cells[layer], router[layer], norms[layer],
            k["middle"], k["second"], k["heads"], tables, weights[layer],
        )
        made = back_rest(
            layer, flag, low, mid, total, norms[layer], k["rows"], k["heads"], weights[layer], following
        )
        grad, more = made[:2]
        if layer:
            sent = made[2]
        grads[layer] = grad
        smalls[layer] = sum_small(jnp.concatenate([small[:8] + more, small[8:]]))
        denses[layer] = images_sum(images_begin(dense_of(k, own_grad, low)))
    denses = [images_end(total) for total in denses]
    input_grad = by_micro(grads[0][:own_rows], grads[1][:own_rows])
    small = by_core(smalls[0], smalls[1])
    mine, theirs = to_layer_owner(denses[0], denses[1])
    dense = jnp.concatenate([by_core(mine, theirs), by_core(theirs, mine)]).astype(f32)
    dense = dense.reshape(4, -1, features)

    def weight_grad(lefts, rights):
        left_own, left_their = to_layer_owner(*lefts)
        right_own, right_their = to_layer_owner(*rights)
        spec = "jrd,jrf->jdf"
        return jnp.einsum(spec, left_own, right_own, preferred_element_type=f32) + jnp.einsum(
            spec, left_their, right_their, preferred_element_type=f32
        )

    grad_first = weight_grad([k["arrived"] for k in kept], inner_grads)
    grad_second = weight_grad([k["hidden"] for k in kept], backs)
    qkv_grad = dense[:3].reshape(3, -1, HEAD_DIM, features)
    return (
        section_out[None, :, None],
        input_grad[None, :, None],
        small[0:2][None],
        small[2:4][None],
        jnp.transpose(qkv_grad, (0, 3, 1, 2))[None],
        dense[3].reshape(w_attn_out.shape),
        small[8 : 8 + experts].T[None],
        grad_first[None],
        grad_second[None],
    )


def solution(mesh):
    return jax.shard_map(
        per_device,
        mesh=mesh,
        in_specs=(
            P(None, "expert", "tensor", None),
            P(None, "expert", "tensor", None),
            P("section", None, None),
            P("section", None, None),
            P("section", None, None, "tensor", None),
            P("section", "tensor", None, None),
            P("section", None, None),
            P("section", "expert", None, "tensor"),
            P("section", "expert", "tensor", None),
            P("section", None, "expert", None, None),
            P("section", None, "expert", None, None),
        ),
        out_specs=(
            P("section", None, "expert", "tensor", None),
            P("section", None, "expert", "tensor", None),
            P("section", None, None),
            P("section", None, None),
            P("section", None, None, "tensor", None),
            P("section", "tensor", None, None),
            P("section", None, None),
            P("section", "expert", None, "tensor"),
            P("section", "expert", "tensor", None),
        ),
        check_vma=False,
    )
```

```python
import functools

import jax
import jax.numpy as jnp
from jax import lax
from jax.experimental import pallas as pl
from jax.experimental.pallas import tpu as pltpu
from jax.sharding import PartitionSpec as P


HEAD_DIM = 64
HEAD_SCALE = 0.125

norm_eps = 1e-06
half_root = 0.7071067811865476
tau_root = 0.3989422804014327
bf16 = jnp.bfloat16
f32 = jnp.float32


def gelu_value(values):
    return 0.5 * values * (1.0 + lax.erf(values * half_root))


def gelu_slope(values):
    return (
        0.5 * (1.0 + lax.erf(values * half_root))
        + values * jnp.exp(-0.5 * values * values) * tau_root
    )


def unit_of(values):
    center = jnp.mean(values, axis=-1, keepdims=True)
    deviation = values - center
    factor = lax.rsqrt(jnp.mean(deviation * deviation, axis=-1, keepdims=True) + norm_eps)
    return deviation * factor, factor


def norm_back(grad_norm, unit_rows, factor, gain_row):
    scaled = grad_norm * gain_row
    return factor * (
        scaled
        - jnp.mean(scaled, axis=-1, keepdims=True)
        - unit_rows * jnp.mean(scaled * unit_rows, axis=-1, keepdims=True)
    )


def dot(left, right):
    return jnp.dot(left, right, preferred_element_type=f32)


def dot_tn(left, right):
    return lax.dot_general(left, right, (((0,), (0,)), ((), ())), preferred_element_type=f32)


def dot_nt(left, right):
    return lax.dot_general(left, right, (((1,), (1,)), ((), ())), preferred_element_type=f32)


def flip(block, axis, mask):
    return lax.ppermute(block, axis, [(i, i ^ mask) for i in range(lax.axis_size(axis))])


def rotate(block, axis, distance):
    count = lax.axis_size(axis)
    return lax.ppermute(block, axis, [(i, (i + distance) % count) for i in range(count)])


def gather_tensor(own):
    return [own] + [flip(own, "tensor", d) for d in range(1, lax.axis_size("tensor"))]


def exchange_tensor(parts):
    return [parts[0]] + [flip(parts[d], "tensor", d) for d in range(1, len(parts))]


def to_owners(blocks):
    return [blocks[0]] + [rotate(blocks[d], "expert", d) for d in range(1, len(blocks))]


def from_owners(blocks):
    return [blocks[0]] + [rotate(blocks[d], "expert", -d) for d in range(1, len(blocks))]


def joined_rows(refs):
    return jnp.concatenate([ref[...] for ref in refs], axis=0)


def lane_mask(head, width):
    lanes = lax.broadcasted_iota(jnp.int32, (1, width), 1)
    return (lanes // HEAD_DIM == head).astype(bf16)


def stack_heads(rows):
    width = rows.shape[1]
    return jnp.concatenate([rows * lane_mask(h, width) for h in range(width // HEAD_DIM)], axis=0)


def fold_heads(stacked):
    width = stacked.shape[1]
    count = width // HEAD_DIM
    size = stacked.shape[0] // count
    total = stacked[:size]
    lanes = lax.broadcasted_iota(jnp.int32, (1, width), 1) // HEAD_DIM
    for head in range(1, count):
        total = jnp.where(lanes == head, stacked[head * size : (head + 1) * size], total)
    return total


def pick_rows(cell_column, count):
    ids = lax.broadcasted_iota(jnp.int32, (cell_column.shape[0], count), 1)
    return ids == cell_column


def pick_cells(cell_row, count):
    ids = lax.broadcasted_iota(jnp.int32, (count, cell_row.shape[1]), 0)
    return ids == cell_row


def expert_sign(pick_column, experts):
    ids = lax.broadcasted_iota(jnp.int32, (pick_column.shape[0], experts), 1)
    return (ids == pick_column).astype(f32)


def combine(middle, gate, cells, table):
    count = table.shape[0]
    first = dot(pick_rows(cells[:, 0:1], count).astype(bf16), table)
    second = dot(pick_rows(cells[:, 1:2], count).astype(bf16), table)
    return middle + gate * first + (1.0 - gate) * second, first - second


def combine_kernel(middle_ref, gate_ref, cells_ref, *refs):
    result_ref, gap_ref = refs[-2:]
    total, gap = combine(
        middle_ref[...], gate_ref[:, 0:1], cells_ref[...], joined_rows(refs[:-2])
    )
    result_ref[...] = total.astype(bf16)
    gap_ref[...] = gap.astype(bf16)


class Weights:
    def __init__(self, layer, flag_ref, refs, held_ref, sems, blocks):
        own, swapped = refs[:2]
        pieces = (len(refs) - 2) // 2
        mine, theirs = refs[2 : 2 + pieces], refs[2 + pieces :]
        width = held_ref.shape[1] // 4
        self.held, self.sems, self.width = held_ref, sems, width
        self.own, self.piece = own, mine[0]
        self.first = blocks[0]
        on_first = flag_ref[0] == 0
        here = flag_ref[0] == layer

        def fetch(source, block, begin, size, sem):
            place = held_ref.at[block - self.first, pl.ds(begin, size)]
            pltpu.make_async_copy(source, place, sems.at[sem]).start()

        def fetch_all(low, high):
            for block in blocks:
                for k in range(2 if block else 0):
                    index = 2 * (block - 1) + k
                    fetch(low[index], block, k * width, width, 4 * (block - 1) + k + 1)
                    fetch(high[index], block, (k + 2) * width, width, 4 * (block - 1) + k + 3)

        if 0 in blocks:

            @pl.when(here)
            def _():
                fetch(own, 0, 0, 4 * width, 0)

            @pl.when(jnp.logical_not(here))
            def _():
                fetch(swapped, 0, 0, 4 * width, 0)

        @pl.when(on_first)
        def _():
            fetch_all(mine, theirs)

        @pl.when(jnp.logical_not(on_first))
        def _():
            fetch_all(theirs, mine)

    def wait(self, block):
        width = self.width
        if isinstance(block, int) and block == 0:
            pltpu.make_async_copy(self.own, self.held.at[0], self.sems.at[0]).wait()
            return
        for k in range(4):
            place = self.held.at[block - self.first, pl.ds(k * width, width)]
            pltpu.make_async_copy(self.piece, place, self.sems.at[4 * (block - 1) + 1 + k]).wait()

    def member(self, block, index):
        return self.held[block - self.first, pl.ds(index * self.width, self.width)]


def front_kernel(layer, joined, tensors, weight_count, *refs):
    refs = list(refs)
    flag_ref = refs.pop(0)
    if joined:
        before_ref, before_gate_ref, before_cells_ref = refs[:3]
        refs = refs[3:]
    table_refs, refs = refs[:tensors], refs[tensors:]
    norms_ref, router_ref, picks_ref, cells_ref = refs[:4]
    weight_refs, refs = refs[4 : 4 + weight_count], refs[4 + weight_count :]
    if joined:
        result_ref, gap_ref = refs[:2]
        refs = refs[2:]
    normed_ref, heads_ref, middle_ref, second_ref, gate_ref, send_ref, held_ref, sems = refs
    weights = Weights(layer, flag_ref, weight_refs, held_ref, sems, range(tensors))
    if joined:
        total, gap = combine(
            before_ref[...], before_gate_ref[:, 0:1], before_cells_ref[...], joined_rows(table_refs)
        )
        low = total.astype(bf16)
        result_ref[...] = low
        gap_ref[...] = gap.astype(bf16)
    else:
        low = joined_rows(table_refs)
    start = low.astype(f32)
    unit, _ = unit_of(start)
    normed_ref[...] = (unit * norms_ref[0:1] + norms_ref[2:3]).astype(bf16)
    middle_ref[...] = start

    def heads_of(block):
        weights.wait(block)
        normed = normed_ref[...]
        query = dot_nt(normed, weights.member(block, 0)).astype(bf16)
        key = dot_nt(normed, weights.member(block, 1)).astype(bf16)
        value = dot_nt(normed, weights.member(block, 2)).astype(bf16)
        raised = jnp.exp(dot_nt(stack_heads(query * HEAD_SCALE), key))
        soft = raised * (1.0 / jnp.sum(raised, axis=-1, keepdims=True))
        attended = fold_heads(dot(soft.astype(bf16), value)).astype(bf16)
        heads_ref[block, 0] = query
        heads_ref[block, 1] = key
        heads_ref[block, 2] = value
        heads_ref[block, 3] = attended
        middle_ref[...] += dot(attended, weights.member(block, 3))

    heads_of(0)

    @pl.loop(1, tensors)
    def _(block):
        heads_of(block)

    unit, _ = unit_of(middle_ref[...])
    second = (unit * norms_ref[1:2] + norms_ref[3:4]).astype(bf16)
    second_ref[...] = second
    logits = dot_nt(second, router_ref[...])
    experts = logits.shape[1]
    sign = expert_sign(picks_ref[:, 0:1], experts) - expert_sign(picks_ref[:, 1:2], experts)
    gap = jnp.sum(sign * logits, axis=-1, keepdims=True)
    gate = 1.0 / (1.0 + jnp.exp(-gap))
    gate_ref[...] = jnp.broadcast_to(gate, gate_ref.shape)
    count = send_ref.shape[0]
    hit = pick_cells(cells_ref[0:1], count) | pick_cells(cells_ref[1:2], count)
    send_ref[...] = dot(hit.astype(bf16), second).astype(bf16)


def spread(grad, gate, cells_row, count):
    wide = grad.astype(f32)
    first = (wide * gate).astype(bf16)
    second = (wide * (1.0 - gate)).astype(bf16)
    total = dot(pick_cells(cells_row[0:1], count).astype(bf16), first)
    total = total + dot(pick_cells(cells_row[1:2], count).astype(bf16), second)
    return total.astype(bf16)


def spread_kernel(gate_ref, cells_ref, *refs):
    grad_refs, (grad_ref, send_ref) = refs[:-2], refs[-2:]
    grad = joined_rows(grad_refs)
    grad_ref[...] = grad
    send_ref[...] = spread(grad, gate_ref[:, 0:1], cells_ref[...], send_ref.shape[0])


def back_heads(weights, block, low, heads_ref, total_ref):
    weights.wait(block)
    out_grad = dot_nt(low, weights.member(block, 3)).astype(bf16)
    query = heads_ref[block, 0]
    key = heads_ref[block, 1]
    value = heads_ref[block, 2]
    count = query.shape[1] // HEAD_DIM
    length = query.shape[0]

    def by_head(stacked):
        return stacked.reshape(count, length, length)

    scaled = query * HEAD_SCALE
    own_keys = stack_heads(key)
    raised = by_head(jnp.exp(dot_nt(own_keys, scaled)))
    probs = raised * (1.0 / jnp.sum(raised, axis=1, keepdims=True))
    prob_grad = by_head(dot_nt(stack_heads(value), out_grad))
    row_dot = jnp.sum(probs * prob_grad, axis=1, keepdims=True)
    score_grad = (probs * (prob_grad - row_dot)).astype(bf16).reshape(count * length, length)
    value_grad = fold_heads(dot(probs.astype(bf16).reshape(count * length, length), out_grad))
    key_grad = fold_heads(dot(score_grad, scaled))
    query_grad = dot_tn(score_grad, own_keys) * HEAD_SCALE
    made = (query_grad.astype(bf16), key_grad.astype(bf16), value_grad.astype(bf16))
    part = dot(made[0], weights.member(block, 0))
    part = part + dot(made[1], weights.member(block, 1)) + dot(made[2], weights.member(block, 2))
    if isinstance(block, int) and block == 0:
        total_ref[...] = part
    else:
        total_ref[...] += part
    return made


def back_open(weights, openers, table_refs, own_ref, low_ref, small_ref, mid_ref, total_ref):
    (
        _,
        grad_ref,
        gap_ref,
        gate_ref,
        picks_ref,
        cells_ref,
        router_ref,
        norms_ref,
        middle_ref,
        second_ref,
        heads_ref,
    ) = openers
    experts = router_ref.shape[0]
    grad = grad_ref[...].astype(f32)
    gate = gate_ref[:, 0:1]
    change = jnp.sum(grad * gap_ref[...].astype(f32), axis=-1, keepdims=True)
    sign = expert_sign(picks_ref[:, 0:1], experts) - expert_sign(picks_ref[:, 1:2], experts)
    logit_grad = (gate * (1.0 - gate) * change * sign).astype(bf16)
    table = joined_rows(table_refs)
    count = table.shape[0]
    hit = pick_rows(cells_ref[:, 0:1], count) | pick_rows(cells_ref[:, 1:2], count)
    normed_grad = dot(hit.astype(bf16), table) + dot(logit_grad, router_ref[...])
    unit, factor = unit_of(middle_ref[...])
    mid = grad + norm_back(normed_grad, unit, factor, norms_ref[1:2])
    small_ref[...] = jnp.zeros_like(small_ref)
    small_ref[1:2] = jnp.sum(normed_grad * unit, axis=0, keepdims=True)
    small_ref[3:4] = jnp.sum(normed_grad, axis=0, keepdims=True)
    small_ref[8 : 8 + experts] = dot_tn(logit_grad, second_ref[...])
    mid_ref[...] = mid
    low = mid.astype(bf16)
    low_ref[...] = low
    made = back_heads(weights, 0, low, heads_ref, total_ref)
    for index in range(3):
        own_ref[index] = made[index]


def back_close(total_ref, start_ref, mid_ref, norms_ref, out_ref, small_ref):
    first_grad = total_ref[...]
    unit, factor = unit_of(start_ref[...].astype(f32))
    small_ref[...] = jnp.zeros_like(small_ref)
    small_ref[0:1] = jnp.sum(first_grad * unit, axis=0, keepdims=True)
    small_ref[2:3] = jnp.sum(first_grad, axis=0, keepdims=True)
    result = (mid_ref[...] + norm_back(first_grad, unit, factor, norms_ref[0:1])).astype(bf16)
    out_ref[...] = result
    return result


def back_first_kernel(layer, tensors, weight_count, *refs):
    refs = list(refs)
    openers, refs = refs[:11], refs[11:]
    table_refs, refs = refs[:tensors], refs[tensors:]
    weight_refs, refs = refs[:weight_count], refs[weight_count:]
    own_ref, low_ref, small_ref, mid_ref, total_ref, held_ref, sems = refs
    weights = Weights(layer, openers[0], weight_refs, held_ref, sems, [0])
    back_open(weights, openers, table_refs, own_ref, low_ref, small_ref, mid_ref, total_ref)


def back_rest_kernel(layer, tensors, weight_count, *refs):
    refs = list(refs)
    flag_ref, low_ref, mid_ref, before_ref, norms_ref, start_ref, heads_ref = refs[:7]
    refs = refs[7:]
    weight_refs, refs = refs[:weight_count], refs[weight_count:]
    out_ref, small_ref, total_ref, held_ref, sems = refs
    weights = Weights(layer, flag_ref, weight_refs, held_ref, sems, range(1, tensors))
    total_ref[...] = before_ref[...]

    @pl.loop(1, tensors)
    def _(block):
        back_heads(weights, block, low_ref[...], heads_ref, total_ref)

    back_close(total_ref, start_ref, mid_ref, norms_ref, out_ref, small_ref)


def back_kernel(layer, tensors, weight_count, *refs):
    refs = list(refs)
    openers, refs = refs[:11], refs[11:]
    table_refs, refs = refs[:tensors], refs[tensors:]
    start_ref, refs = refs[0], refs[1:]
    weight_refs, refs = refs[:weight_count], refs[weight_count:]
    next_gate_ref, next_cells_ref = refs[:2]
    own_ref, low_ref, small_ref, out_ref, more_ref, send_ref, mid_ref, total_ref, held_ref, sems = refs[2:]
    norms_ref, heads_ref = openers[7], openers[10]
    weights = Weights(layer, openers[0], weight_refs, held_ref, sems, range(tensors))
    back_open(weights, openers, table_refs, own_ref, low_ref, small_ref, mid_ref, total_ref)

    @pl.loop(1, tensors)
    def _(block):
        back_heads(weights, block, low_ref[...], heads_ref, total_ref)

    result = back_close(total_ref, start_ref, mid_ref, norms_ref, out_ref, more_ref)
    send_ref[...] = spread(result, next_gate_ref[:, 0:1], next_cells_ref[...], send_ref.shape[0])


def with_either(chosen, own_refs, their_refs, body):
    @pl.when(chosen)
    def _():
        body(*own_refs)

    @pl.when(jnp.logical_not(chosen))
    def _():
        body(*their_refs)


def expert_kernel(layer, tensors, flag_ref, *refs):
    row_refs, refs = refs[:tensors], refs[tensors:]
    own_refs, their_refs, refs = refs[:2], refs[2:4], refs[4:]
    out_refs, (packed_ref, hidden_ref, slope_ref) = refs[:tensors], refs[tensors:]

    def body(first_ref, second_ref):
        rows = jnp.concatenate([ref[0] for ref in row_refs], axis=0)
        packed_ref[0] = rows
        inner = dot(rows, first_ref[0])
        hidden = gelu_value(inner).astype(bf16)
        hidden_ref[0] = hidden
        slope_ref[0] = gelu_slope(inner).astype(bf16)
        outer = dot(hidden, second_ref[0]).astype(bf16)
        size = outer.shape[0] // tensors
        for d in range(tensors):
            out_refs[d][0] = outer[d * size : (d + 1) * size]

    with_either(flag_ref[0] == layer, own_refs, their_refs, body)


def expert_back_kernel(layer, tensors, flag_ref, *refs):
    row_refs, refs = refs[:tensors], refs[tensors:]
    slope_ref = refs[0]
    own_refs, their_refs, refs = refs[1:3], refs[3:5], refs[5:]
    out_refs, (packed_ref, inner_ref) = refs[:tensors], refs[tensors:]

    def body(first_ref, second_ref):
        rows = jnp.concatenate([ref[0] for ref in row_refs], axis=0)
        packed_ref[0] = rows
        inner_grad = (dot_nt(rows, second_ref[0]) * slope_ref[0].astype(f32)).astype(bf16)
        inner_ref[0] = inner_grad
        outer = dot_nt(inner_grad, first_ref[0]).astype(bf16)
        size = outer.shape[0] // tensors
        for d in range(tensors):
            out_refs[d][0] = outer[d * size : (d + 1) * size]

    with_either(flag_ref[0] == layer, own_refs, their_refs, body)


def shaped(shape, dtype):
    return jax.ShapeDtypeStruct(shape, dtype)


def cost_of(flops, byte_count):
    return pl.CostEstimate(flops=flops, bytes_accessed=byte_count, transcendentals=0)


LIMIT = 48 * 1024 * 1024
IN_VMEM = pl.BlockSpec(memory_space=pltpu.VMEM)
IN_SMEM = pl.BlockSpec(memory_space=pltpu.SMEM)
ANYWHERE = pl.BlockSpec(memory_space=pl.ANY)


def run_kernel(kernel, args, kinds, outs, scratch=(), cost=None):
    return pl.pallas_call(
        kernel,
        in_specs=[kinds.get(i, IN_VMEM) for i in range(len(args))],
        out_specs=[IN_VMEM] * len(outs),
        out_shape=outs,
        scratch_shapes=list(scratch),
        cost_estimate=cost,
        compiler_params=pltpu.CompilerParams(vmem_limit_bytes=LIMIT),
    )(*args)


def weight_scratch(weights, blocks, tensors):
    rows, features = weights[0].shape
    return [
        pltpu.VMEM((blocks, rows, features), bf16),
        pltpu.SemaphoreType.DMA((4 * tensors - 3,)),
    ]


def front(layer, flag, start, tables, norms, router, picks, cells_row, weights, share):
    joined = start is not None
    tensors = len(tables)
    length = picks.shape[0]
    rows, features = weights[0].shape
    rows_low = shaped((length, features), bf16)
    outs = [rows_low, rows_low] if joined else []
    outs = outs + [
        rows_low,
        shaped((tensors, 4, length, rows // 4), bf16),
        shaped((length, features), f32),
        rows_low,
        shaped((length, 128), f32),
        shaped((share, features), bf16),
    ]
    args = [flag] + list(start or ()) + list(tables) + [norms, router, picks, cells_row]
    kinds = {0: IN_SMEM}
    kinds.update({len(args) + i: ANYWHERE for i in range(len(weights))})
    return run_kernel(
        functools.partial(front_kernel, layer, joined, tensors, len(weights)),
        args + list(weights),
        kinds,
        outs,
        weight_scratch(weights, tensors, tensors),
        cost_of(3_000_000_000, 9_000_000),
    )


def join(middle, gate, cells, tables):
    rows_low = shaped(middle.shape, bf16)
    return run_kernel(
        combine_kernel, [middle, gate, cells] + list(tables), {}, [rows_low, rows_low],
        cost=cost_of(800_000_000, 3_000_000),
    )


def spread_rows(gate, cells_row, grads, share):
    length = gate.shape[0]
    features = grads[0].shape[1]
    outs = [shaped((length, features), bf16), shaped((share, features), bf16)]
    return run_kernel(
        spread_kernel, [gate, cells_row] + list(grads), {}, outs, cost=cost_of(100_000_000, 1_000_000)
    )


def back_first(layer, openers, tables, weights):
    length, features = openers[1].shape
    tensors = len(tables)
    width = openers[10].shape[3]
    experts = openers[6].shape[0]
    args = list(openers) + list(tables)
    kinds = {0: IN_SMEM}
    kinds.update({len(args) + i: ANYWHERE for i in range(len(weights))})
    wide = shaped((length, features), f32)
    outs = [
        shaped((3, length, width), bf16),
        shaped((length, features), bf16),
        shaped((8 + experts, features), f32),
        wide,
        wide,
    ]
    return run_kernel(
        functools.partial(back_first_kernel, layer, tensors, len(weights)),
        args + list(weights),
        kinds,
        outs,
        weight_scratch(weights, 1, tensors),
        cost_of(2_000_000_000, 6_000_000),
    )


def back_rest(layer, flag, low, mid, total, norms, start, heads, weights):
    length, features = low.shape
    tensors = heads.shape[0]
    args = [flag, low, mid, total, norms, start, heads]
    kinds = {0: IN_SMEM}
    kinds.update({len(args) + i: ANYWHERE for i in range(len(weights))})
    return run_kernel(
        functools.partial(back_rest_kernel, layer, tensors, len(weights)),
        args + list(weights),
        kinds,
        [shaped((length, features), bf16), shaped((8, features), f32)],
        [pltpu.VMEM((length, features), f32)] + weight_scratch(weights, tensors - 1, tensors),
        cost_of(4_000_000_000, 9_000_000),
    )


def back(layer, openers, tables, start, weights, next_gate, next_cells, share):
    length, features = openers[1].shape
    tensors = len(tables)
    width = openers[10].shape[3]
    experts = openers[6].shape[0]
    args = list(openers) + list(tables) + [start]
    kinds = {0: IN_SMEM}
    kinds.update({len(args) + i: ANYWHERE for i in range(len(weights))})
    args = args + list(weights) + [next_gate, next_cells]
    rows_low = shaped((length, features), bf16)
    wide = pltpu.VMEM((length, features), f32)
    return run_kernel(
        functools.partial(back_kernel, layer, tensors, len(weights)),
        args,
        kinds,
        [
            shaped((3, length, width), bf16),
            rows_low,
            shaped((8 + experts, features), f32),
            rows_low,
            shaped((8, features), f32),
            shaped((share, features), bf16),
        ],
        [wide, wide] + weight_scratch(weights, tensors, tensors),
        cost_of(5_000_000_000, 12_000_000),
    )


def run_experts(kernel, layer, flag, rows, more, own, theirs, extra):
    local, _, _ = rows[0].shape
    tensors = len(rows)

    def block(shape):
        return pl.BlockSpec((1,) + tuple(shape[1:]), lambda j, flag_ref: (j, 0, 0))

    def weight(shape, wanted):
        def index(j, flag_ref):
            return (jnp.where((flag_ref[0] == layer) == wanted, j, 0), 0, 0)

        return pl.BlockSpec((1,) + tuple(shape[1:]), index)

    args = list(rows) + list(more)
    specs = [block(a.shape) for a in args]
    specs = specs + [weight(w.shape, True) for w in own] + [weight(w.shape, False) for w in theirs]
    outs = [shaped(r.shape, bf16) for r in rows] + list(extra)
    return pl.pallas_call(
        functools.partial(kernel, layer, tensors),
        grid_spec=pltpu.PrefetchScalarGridSpec(
            num_scalar_prefetch=1,
            grid=(local,),
            in_specs=specs,
            out_specs=[block(o.shape) for o in outs],
        ),
        out_shape=outs,
        cost_estimate=cost_of(1_200_000_000, 9_000_000),
        compiler_params=pltpu.CompilerParams(
            dimension_semantics=("arbitrary",), vmem_limit_bytes=LIMIT
        ),
    )(flag, *args, *own, *theirs)


def per_device(
    tokens,
    cotangent,
    norm_gains,
    norm_shifts,
    w_qkv,
    w_attn_out,
    w_router,
    w_in,
    w_out,
    choices,
    slot_ranks,
):
    section = lax.axis_index("section")
    tensor = lax.axis_index("tensor")
    here = lax.axis_index("expert")
    tensors = lax.axis_size("tensor")
    owners = lax.axis_size("expert")
    features = tokens.shape[3]
    own_rows = tokens.shape[2]
    length = choices.shape[3]
    experts = w_router.shape[2]
    local = w_in.shape[1]
    hidden_count = w_in.shape[3]
    capacity = 2 * length // experts
    part = capacity // tensors
    share = experts * part
    on_first = section == 0
    flag = section.astype(jnp.int32).reshape(1)

    def swap(block):
        return flip(block, "section", 1)

    def both_layers(block):
        theirs = swap(block)
        return [jnp.where(section == layer, block, theirs) for layer in range(2)]

    def by_core(first, second):
        return jnp.where(on_first, first, second)

    own_weight = jnp.concatenate(
        [
            jnp.transpose(w_qkv[0], (0, 2, 3, 1)).reshape(-1, features),
            w_attn_out[0].reshape(-1, features),
        ]
    )
    swapped_weight = swap(own_weight)
    half = own_weight.shape[0] // 2

    def all_heads(layer):
        if layer == 0:
            piece = by_core(own_weight[:half], swapped_weight[half:])
        else:
            piece = by_core(swapped_weight[:half], own_weight[half:])
        one, two = piece[: half // 2], piece[half // 2 :]
        one_x, two_y = flip(one, "tensor", 1), flip(two, "tensor", 2)
        one_y, two_x = flip(one, "tensor", 2), flip(two, "tensor", 1)
        one_far, two_far = flip(one_x, "tensor", 2), flip(two_y, "tensor", 1)
        mine = [one_x, two_x, one_y, two_y, one_far, two_far]
        return [own_weight, swapped_weight] + mine + [swap(block) for block in mine]

    weights = [all_heads(0), all_heads(1)]
    rows = gather_tensor(by_core(tokens[0, 0], tokens[1, 0]))

    order = jnp.arange(tensors) ^ tensor
    table = jnp.stack([choices[0, :, 0], slot_ranks[0, :, 0]], axis=1)
    table = jnp.swapaxes(table, 2, 3)
    mine = by_core(table[0], table[1])
    theirs = swap(by_core(table[1], table[0]))
    picks, cells, cells_row = [], [], []
    for layer in range(2):
        route = jnp.where(section == layer, mine, theirs)
        route = route.reshape(2, 2, tensors, own_rows)[:, :, order].reshape(2, 2, length)
        pick, slot = route[0], route[1]
        owner = (pick // local - here) % owners
        block = (slot // part) ^ tensor
        cell = block * share + (owner * local + pick % local) * part + slot % part
        cell = jnp.where(slot < capacity, cell, tensors * share)
        picks.append(pick.T)
        cells.append(cell.T)
        cells_row.append(cell)

    norms = both_layers(jnp.concatenate([norm_gains[0], norm_shifts[0]]))
    router = both_layers(w_router[0].T)
    own_experts = (w_in[0], w_out[0])
    their_experts = (swap(w_in[0]), swap(w_out[0]))

    def send_out(sent):
        arrived = to_owners(list(sent.reshape(owners, local, part, features)))
        return gather_tensor(jnp.concatenate(arrived, axis=1))

    def bring_back(parts):
        came = exchange_tensor(parts)
        total = came[0].astype(f32)
        for one in came[1:]:
            total = total + one.astype(f32)
        total = total.astype(bf16)
        blocks = [total[:, s * part : (s + 1) * part].reshape(-1, features) for s in range(owners)]
        return gather_tensor(jnp.concatenate(from_owners(blocks)))

    packed = shaped((local, tensors * owners * part, features), bf16)
    packed_hidden = shaped((local, tensors * owners * part, hidden_count), bf16)
    kept = []
    start, tables = None, rows
    for layer in range(2):
        made = front(
            layer, flag, start, tables, norms[layer], router[layer], picks[layer], cells_row[layer],
            weights[layer], share,
        )
        if layer:
            kept[0]["result"], kept[0]["gap"] = made[:2]
            base = made[0]
            made = made[2:]
        else:
            base = jnp.concatenate(rows)
        normed, heads, middle, second, gate, sent = made
        arrived = send_out(sent)
        done = run_experts(
            expert_kernel, layer, flag, arrived, (), own_experts, their_experts,
            (packed, packed_hidden, packed_hidden),
        )
        tables = bring_back(done[:tensors])
        start = (middle, gate, cells[layer])
        kept.append(
            dict(
                rows=base, normed=normed, heads=heads, middle=middle, second=second, gate=gate,
                arrived=done[tensors], hidden=done[tensors + 1], slope=done[tensors + 2],
            )
        )
    kept[1]["result"], kept[1]["gap"] = join(*start, tables)

    def to_layer_owner(first_layer, second_layer):
        return by_core(first_layer, second_layer), swap(by_core(second_layer, first_layer))

    def by_micro(first_layer, second_layer):
        mine, theirs = to_layer_owner(first_layer, second_layer)
        return jnp.stack([by_core(mine, theirs), by_core(theirs, mine)])

    section_out = by_micro(kept[0]["result"][:own_rows], kept[1]["result"][:own_rows])

    def images_begin(block):
        size = block.shape[0] // 2
        mine = by_core(block[:size], block[size:])
        theirs = swap(by_core(block[size:], block[:size]))
        total = (mine.astype(f32) + theirs.astype(f32)).astype(bf16)
        return total.reshape(owners, -1, features)

    def images_sum(parts):
        total = lax.dynamic_index_in_dim(parts, here, 0, keepdims=False).astype(f32)
        for d in range(1, owners):
            piece = lax.dynamic_index_in_dim(parts, (here + d) % owners, 0, keepdims=False)
            came = rotate(piece, "expert", d)
            total = total + came.astype(f32)
        return total.astype(bf16)

    def images_end(total):
        others = [rotate(total, "expert", -d) for d in range(1, owners)]
        held = jnp.stack([total] + others)
        return jnp.roll(held, here, axis=0).reshape(-1, features)

    def sum_small(first_layer, second_layer):
        small = by_core(first_layer, second_layer) + swap(by_core(second_layer, first_layer))
        step = 1
        while step < owners:
            small = small + flip(small, "expert", step)
            step *= 2
        return small

    def dense_of(kept_layer, own_grad, low):
        pieces = [dot_tn(own_grad[member], kept_layer["normed"]) for member in range(3)]
        pieces.append(dot_tn(kept_layer["heads"][0, 3], low))
        return jnp.concatenate([piece.astype(bf16) for piece in pieces])

    gathered = gather_tensor(by_core(cotangent[0, 0], cotangent[1, 0]).astype(bf16))
    grad, sent = spread_rows(kept[1]["gate"], cells_row[1], gathered, share)
    grads, smalls, denses, backs, inner_grads = [None] * 2, [None] * 2, [None] * 2, [None] * 2, [None] * 2
    for layer in (1, 0):
        k = kept[layer]
        came = send_out(sent)
        done = run_experts(
            expert_back_kernel, layer, flag, came, (k["slope"],), own_experts, their_experts,
            (packed, packed_hidden),
        )
        backs[layer], inner_grads[layer] = done[tensors:]
        tables = bring_back(done[:tensors])
        openers = [
            flag, grad, k["gap"], k["gate"], picks[layer], cells[layer], router[layer], norms[layer],
            k["middle"], k["second"], k["heads"],
        ]
        if layer:
            own_grad, low, small, grad, more, sent = back(
                layer, openers, tables, k["rows"], weights[layer], kept[0]["gate"], cells_row[0], share
            )
        else:
            own_grad, low, small, mid, total = back_first(layer, openers, tables, weights[layer])
            grad, more = back_rest(
                layer, flag, low, mid, total, norms[layer], k["rows"], k["heads"], weights[layer]
            )
        grads[layer] = grad
        smalls[layer] = jnp.concatenate([small[:8] + more, small[8:]])
        denses[layer] = images_sum(images_begin(dense_of(k, own_grad, low)))
    denses = [images_end(total) for total in denses]
    input_grad = by_micro(grads[0][:own_rows], grads[1][:own_rows])
    small = sum_small(*smalls)
    mine, theirs = to_layer_owner(denses[0], denses[1])
    dense = jnp.concatenate([by_core(mine, theirs), by_core(theirs, mine)]).astype(f32)
    dense = dense.reshape(4, -1, features)

    def weight_grad(lefts, rights):
        left_own, left_their = to_layer_owner(*lefts)
        right_own, right_their = to_layer_owner(*rights)
        spec = "jrd,jrf->jdf"
        return jnp.einsum(spec, left_own, right_own, preferred_element_type=f32) + jnp.einsum(
            spec, left_their, right_their, preferred_element_type=f32
        )

    grad_first = weight_grad([k["arrived"] for k in kept], inner_grads)
    grad_second = weight_grad([k["hidden"] for k in kept], backs)
    qkv_grad = dense[:3].reshape(3, -1, HEAD_DIM, features)
    return (
        section_out[None, :, None],
        input_grad[None, :, None],
        small[0:2][None],
        small[2:4][None],
        jnp.transpose(qkv_grad, (0, 3, 1, 2))[None],
        dense[3].reshape(w_attn_out.shape),
        small[8 : 8 + experts].T[None],
        grad_first[None],
        grad_second[None],
    )


def solution(mesh):
    return jax.shard_map(
        per_device,
        mesh=mesh,
        in_specs=(
            P(None, "expert", "tensor", None),
            P(None, "expert", "tensor", None),
            P("section", None, None),
            P("section", None, None),
            P("section", None, None, "tensor", None),
            P("section", "tensor", None, None),
            P("section", None, None),
            P("section", "expert", None, "tensor"),
            P("section", "expert", "tensor", None),
            P("section", None, "expert", None, None),
            P("section", None, "expert", None, None),
        ),
        out_specs=(
            P("section", None, "expert", "tensor", None),
            P("section", None, "expert", "tensor", None),
            P("section", None, None),
            P("section", None, None),
            P("section", None, None, "tensor", None),
            P("section", "tensor", None, None),
            P("section", None, None),
            P("section", "expert", None, "tensor"),
            P("section", "expert", "tensor", None),
        ),
        check_vma=False,
    )
```

```python
import functools

import jax
import jax.numpy as jnp
from jax import lax
from jax.experimental import pallas as pl
from jax.experimental.pallas import tpu as pltpu
from jax.sharding import PartitionSpec as P


HEAD_DIM = 64
HEAD_SCALE = 0.125

norm_eps = 1e-06
half_root = 0.7071067811865476
tau_root = 0.3989422804014327
bf16 = jnp.bfloat16
f32 = jnp.float32


def gelu_value(values):
    return 0.5 * values * (1.0 + lax.erf(values * half_root))


def gelu_slope(values):
    return (
        0.5 * (1.0 + lax.erf(values * half_root))
        + values * jnp.exp(-0.5 * values * values) * tau_root
    )


def unit_of(values):
    center = jnp.mean(values, axis=-1, keepdims=True)
    deviation = values - center
    factor = lax.rsqrt(jnp.mean(deviation * deviation, axis=-1, keepdims=True) + norm_eps)
    return deviation * factor, factor


def norm_back(grad_norm, unit_rows, factor, gain_row):
    scaled = grad_norm * gain_row
    return factor * (
        scaled
        - jnp.mean(scaled, axis=-1, keepdims=True)
        - unit_rows * jnp.mean(scaled * unit_rows, axis=-1, keepdims=True)
    )


def dot(left, right):
    return jnp.dot(left, right, preferred_element_type=f32)


def dot_tn(left, right):
    return lax.dot_general(left, right, (((0,), (0,)), ((), ())), preferred_element_type=f32)


def dot_nt(left, right):
    return lax.dot_general(left, right, (((1,), (1,)), ((), ())), preferred_element_type=f32)


def flip(block, axis, mask):
    return lax.ppermute(block, axis, [(i, i ^ mask) for i in range(lax.axis_size(axis))])


def rotate(block, axis, distance):
    count = lax.axis_size(axis)
    return lax.ppermute(block, axis, [(i, (i + distance) % count) for i in range(count)])


def gather_tensor(own):
    return [own] + [flip(own, "tensor", d) for d in range(1, lax.axis_size("tensor"))]


def exchange_tensor(parts):
    return [parts[0]] + [flip(parts[d], "tensor", d) for d in range(1, len(parts))]


def to_owners(blocks):
    return [blocks[0]] + [rotate(blocks[d], "expert", d) for d in range(1, len(blocks))]


def from_owners(blocks):
    return [blocks[0]] + [rotate(blocks[d], "expert", -d) for d in range(1, len(blocks))]


def joined_rows(refs):
    return jnp.concatenate([ref[...] for ref in refs], axis=0)


def lane_mask(head, width):
    lanes = lax.broadcasted_iota(jnp.int32, (1, width), 1)
    return (lanes // HEAD_DIM == head).astype(bf16)


def stack_heads(rows):
    width = rows.shape[1]
    return jnp.concatenate([rows * lane_mask(h, width) for h in range(width // HEAD_DIM)], axis=0)


def fold_heads(stacked):
    width = stacked.shape[1]
    count = width // HEAD_DIM
    size = stacked.shape[0] // count
    total = stacked[:size]
    lanes = lax.broadcasted_iota(jnp.int32, (1, width), 1) // HEAD_DIM
    for head in range(1, count):
        total = jnp.where(lanes == head, stacked[head * size : (head + 1) * size], total)
    return total


def pick_rows(cell_column, count):
    ids = lax.broadcasted_iota(jnp.int32, (cell_column.shape[0], count), 1)
    return ids == cell_column


def pick_cells(cell_row, count):
    ids = lax.broadcasted_iota(jnp.int32, (count, cell_row.shape[1]), 0)
    return ids == cell_row


def expert_sign(pick_column, experts):
    ids = lax.broadcasted_iota(jnp.int32, (pick_column.shape[0], experts), 1)
    return (ids == pick_column).astype(f32)


def combine(middle, gate, cells, table):
    count = table.shape[0]
    first = dot(pick_rows(cells[:, 0:1], count).astype(bf16), table)
    second = dot(pick_rows(cells[:, 1:2], count).astype(bf16), table)
    return middle + gate * first + (1.0 - gate) * second, first - second


def combine_kernel(middle_ref, gate_ref, cells_ref, *refs):
    result_ref, gap_ref = refs[-2:]
    total, gap = combine(
        middle_ref[...], gate_ref[:, 0:1], cells_ref[...], joined_rows(refs[:-2])
    )
    result_ref[...] = total.astype(bf16)
    gap_ref[...] = gap.astype(bf16)


class Weights:
    def __init__(self, layer, flag_ref, refs, held_ref, sems, blocks):
        own, swapped = refs[:2]
        pieces = (len(refs) - 2) // 2
        mine, theirs = refs[2 : 2 + pieces], refs[2 + pieces :]
        width = held_ref.shape[1] // 4
        self.held, self.sems, self.width = held_ref, sems, width
        self.piece = mine[0]
        self.first = blocks[0]
        on_first = flag_ref[0] == 0
        here = flag_ref[0] == layer

        def fetch(source, block, k):
            place = held_ref.at[block - self.first, pl.ds(k * width, width)]
            pltpu.make_async_copy(source, place, sems.at[4 * block + k]).start()

        def fetch_own(source):
            for k in range(4):
                fetch(source.at[pl.ds(k * width, width)], 0, k)

        def fetch_all(low, high):
            for block in blocks:
                for k in range(2 if block else 0):
                    index = 2 * (block - 1) + k
                    fetch(low[index], block, k)
                    fetch(high[index], block, k + 2)

        if 0 in blocks:

            @pl.when(here)
            def _():
                fetch_own(own)

            @pl.when(jnp.logical_not(here))
            def _():
                fetch_own(swapped)

        @pl.when(on_first)
        def _():
            fetch_all(mine, theirs)

        @pl.when(jnp.logical_not(on_first))
        def _():
            fetch_all(theirs, mine)

    def wait(self, block):
        for k in range(4):
            place = self.held.at[block - self.first, pl.ds(k * self.width, self.width)]
            pltpu.make_async_copy(self.piece, place, self.sems.at[4 * block + k]).wait()

    def member(self, block, index):
        return self.held[block - self.first, pl.ds(index * self.width, self.width)]


def front_kernel(layer, joined, tensors, weight_count, *refs):
    refs = list(refs)
    flag_ref = refs.pop(0)
    if joined:
        before_ref, before_gate_ref, before_cells_ref = refs[:3]
        refs = refs[3:]
    table_refs, refs = refs[:tensors], refs[tensors:]
    norms_ref, router_ref, picks_ref, cells_ref = refs[:4]
    weight_refs, refs = refs[4 : 4 + weight_count], refs[4 + weight_count :]
    if joined:
        result_ref, gap_ref = refs[:2]
        refs = refs[2:]
    normed_ref, heads_ref, middle_ref, second_ref, gate_ref, send_ref, held_ref, sems = refs
    weights = Weights(layer, flag_ref, weight_refs, held_ref, sems, range(tensors))
    if joined:
        total, gap = combine(
            before_ref[...], before_gate_ref[:, 0:1], before_cells_ref[...], joined_rows(table_refs)
        )
        low = total.astype(bf16)
        result_ref[...] = low
        gap_ref[...] = gap.astype(bf16)
    else:
        low = joined_rows(table_refs)
    start = low.astype(f32)
    unit, _ = unit_of(start)
    normed_ref[...] = (unit * norms_ref[0:1] + norms_ref[2:3]).astype(bf16)
    middle_ref[...] = start

    def heads_of(block):
        weights.wait(block)
        normed = normed_ref[...]
        query = dot_nt(normed, weights.member(block, 0)).astype(bf16)
        key = dot_nt(normed, weights.member(block, 1)).astype(bf16)
        value = dot_nt(normed, weights.member(block, 2)).astype(bf16)
        scores = dot_nt(stack_heads(query * HEAD_SCALE), key)
        soft = jnp.exp(scores - jnp.log(jnp.sum(jnp.exp(scores), axis=-1, keepdims=True)))
        attended = fold_heads(dot(soft.astype(bf16), value)).astype(bf16)
        heads_ref[block, 0] = query
        heads_ref[block, 1] = key
        heads_ref[block, 2] = value
        heads_ref[block, 3] = attended
        middle_ref[...] += dot(attended, weights.member(block, 3))

    heads_of(0)

    @pl.loop(1, tensors)
    def _(block):
        heads_of(block)

    unit, _ = unit_of(middle_ref[...])
    second = (unit * norms_ref[1:2] + norms_ref[3:4]).astype(bf16)
    second_ref[...] = second
    logits = dot_nt(second, router_ref[...])
    experts = logits.shape[1]
    sign = expert_sign(picks_ref[:, 0:1], experts) - expert_sign(picks_ref[:, 1:2], experts)
    gap = jnp.sum(sign * logits, axis=-1, keepdims=True)
    gate = 1.0 / (1.0 + jnp.exp(-gap))
    gate_ref[...] = jnp.broadcast_to(gate, gate_ref.shape)
    count = send_ref.shape[0]
    hit = pick_cells(cells_ref[0:1], count) | pick_cells(cells_ref[1:2], count)
    send_ref[...] = dot(hit.astype(bf16), second).astype(bf16)


def spread(grad, gate, cells_row, count):
    wide = grad.astype(f32)
    first = (wide * gate).astype(bf16)
    second = (wide * (1.0 - gate)).astype(bf16)
    total = dot(pick_cells(cells_row[0:1], count).astype(bf16), first)
    total = total + dot(pick_cells(cells_row[1:2], count).astype(bf16), second)
    return total.astype(bf16)


def spread_kernel(gate_ref, cells_ref, *refs):
    grad_refs, (grad_ref, send_ref) = refs[:-2], refs[-2:]
    grad = joined_rows(grad_refs)
    grad_ref[...] = grad
    send_ref[...] = spread(grad, gate_ref[:, 0:1], cells_ref[...], send_ref.shape[0])


def back_heads(weights, block, low, heads_ref, total_ref):
    weights.wait(block)
    out_grad = dot_nt(low, weights.member(block, 3)).astype(bf16)
    query = heads_ref[block, 0]
    key = heads_ref[block, 1]
    value = heads_ref[block, 2]
    count = query.shape[1] // HEAD_DIM
    length = query.shape[0]

    def by_head(stacked):
        return stacked.reshape(count, length, length)

    scaled = query * HEAD_SCALE
    own_keys = stack_heads(key)
    scores = by_head(dot_nt(own_keys, scaled))
    probs = jnp.exp(scores - jnp.log(jnp.sum(jnp.exp(scores), axis=1, keepdims=True)))
    prob_grad = by_head(dot_nt(stack_heads(value), out_grad))
    row_dot = jnp.sum(probs * prob_grad, axis=1, keepdims=True)
    score_grad = (probs * (prob_grad - row_dot)).astype(bf16).reshape(count * length, length)
    value_grad = fold_heads(dot(probs.astype(bf16).reshape(count * length, length), out_grad))
    key_grad = fold_heads(dot(score_grad, scaled))
    query_grad = dot_tn(score_grad, own_keys) * HEAD_SCALE
    made = (query_grad.astype(bf16), key_grad.astype(bf16), value_grad.astype(bf16))
    part = dot(made[0], weights.member(block, 0))
    part = part + dot(made[1], weights.member(block, 1)) + dot(made[2], weights.member(block, 2))
    if isinstance(block, int):
        total_ref[...] = part
    else:
        total_ref[...] += part
    return made


def back_open(openers, table_refs, low_ref, small_ref, mid_ref):
    (
        _,
        grad_ref,
        gap_ref,
        gate_ref,
        picks_ref,
        cells_ref,
        router_ref,
        norms_ref,
        middle_ref,
        second_ref,
        _,
    ) = openers
    experts = router_ref.shape[0]
    grad = grad_ref[...].astype(f32)
    gate = gate_ref[:, 0:1]
    change = jnp.sum(grad * gap_ref[...].astype(f32), axis=-1, keepdims=True)
    sign = expert_sign(picks_ref[:, 0:1], experts) - expert_sign(picks_ref[:, 1:2], experts)
    logit_grad = (gate * (1.0 - gate) * change * sign).astype(bf16)
    table = joined_rows(table_refs)
    count = table.shape[0]
    hit = pick_rows(cells_ref[:, 0:1], count) | pick_rows(cells_ref[:, 1:2], count)
    normed_grad = dot(hit.astype(bf16), table) + dot(logit_grad, router_ref[...])
    unit, factor = unit_of(middle_ref[...])
    mid = grad + norm_back(normed_grad, unit, factor, norms_ref[1:2])
    small_ref[...] = jnp.zeros_like(small_ref)
    small_ref[1:2] = jnp.sum(normed_grad * unit, axis=0, keepdims=True)
    small_ref[3:4] = jnp.sum(normed_grad, axis=0, keepdims=True)
    small_ref[8 : 8 + experts] = dot_tn(logit_grad, second_ref[...])
    mid_ref[...] = mid
    low = mid.astype(bf16)
    low_ref[...] = low


def keep_own(own_ref, made):
    for index in range(3):
        own_ref[index] = made[index]


def back_close(total_ref, start_ref, mid_ref, norms_ref, out_ref, small_ref):
    first_grad = total_ref[...]
    unit, factor = unit_of(start_ref[...].astype(f32))
    small_ref[...] = jnp.zeros_like(small_ref)
    small_ref[0:1] = jnp.sum(first_grad * unit, axis=0, keepdims=True)
    small_ref[2:3] = jnp.sum(first_grad, axis=0, keepdims=True)
    result = (mid_ref[...] + norm_back(first_grad, unit, factor, norms_ref[0:1])).astype(bf16)
    out_ref[...] = result
    return result


def back_first_kernel(layer, tensors, weight_count, *refs):
    refs = list(refs)
    openers, refs = refs[:11], refs[11:]
    table_refs, refs = refs[:tensors], refs[tensors:]
    weight_refs, refs = refs[:weight_count], refs[weight_count:]
    own_ref, low_ref, small_ref, mid_ref, total_ref, held_ref, sems = refs
    weights = Weights(layer, openers[0], weight_refs, held_ref, sems, [0])
    back_open(openers, table_refs, low_ref, small_ref, mid_ref)
    keep_own(own_ref, back_heads(weights, 0, low_ref[...], openers[10], total_ref))


def back_rest_kernel(layer, tensors, weight_count, *refs):
    refs = list(refs)
    flag_ref, low_ref, mid_ref, before_ref, norms_ref, start_ref, heads_ref = refs[:7]
    refs = refs[7:]
    weight_refs, refs = refs[:weight_count], refs[weight_count:]
    out_ref, small_ref, total_ref, held_ref, sems = refs
    weights = Weights(layer, flag_ref, weight_refs, held_ref, sems, range(1, tensors))
    total_ref[...] = before_ref[...]

    @pl.loop(1, tensors)
    def _(block):
        back_heads(weights, block, low_ref[...], heads_ref, total_ref)

    back_close(total_ref, start_ref, mid_ref, norms_ref, out_ref, small_ref)


def back_kernel(layer, tensors, weight_count, *refs):
    refs = list(refs)
    openers, refs = refs[:11], refs[11:]
    table_refs, refs = refs[:tensors], refs[tensors:]
    start_ref, refs = refs[0], refs[1:]
    weight_refs, refs = refs[:weight_count], refs[weight_count:]
    next_gate_ref, next_cells_ref = refs[:2]
    own_ref, low_ref, small_ref, out_ref, more_ref, send_ref, mid_ref, total_ref, held_ref, sems = refs[2:]
    norms_ref, heads_ref = openers[7], openers[10]
    weights = Weights(layer, openers[0], weight_refs, held_ref, sems, range(tensors))
    back_open(openers, table_refs, low_ref, small_ref, mid_ref)

    keep_own(own_ref, back_heads(weights, 0, low_ref[...], heads_ref, total_ref))

    @pl.loop(1, tensors)
    def _(block):
        back_heads(weights, block, low_ref[...], heads_ref, total_ref)

    result = back_close(total_ref, start_ref, mid_ref, norms_ref, out_ref, more_ref)
    send_ref[...] = spread(result, next_gate_ref[:, 0:1], next_cells_ref[...], send_ref.shape[0])


def back_kernel(layer, tensors, weight_count, *refs):
    refs = list(refs)
    openers, refs = refs[:11], refs[11:]
    table_refs, refs = refs[:tensors], refs[tensors:]
    start_ref, refs = refs[0], refs[1:]
    weight_refs, refs = refs[:weight_count], refs[weight_count:]
    next_gate_ref, next_cells_ref = refs[:2]
    own_ref, low_ref, small_ref, out_ref, more_ref, send_ref, mid_ref, total_ref, held_ref, sems = refs[2:]
    norms_ref, heads_ref = openers[7], openers[10]
    weights = Weights(layer, openers[0], weight_refs, held_ref, sems, range(tensors))
    back_open(openers, table_refs, low_ref, small_ref, mid_ref)

    keep_own(own_ref, back_heads(weights, 0, low_ref[...], heads_ref, total_ref))

    @pl.loop(1, tensors)
    def _(block):
        back_heads(weights, block, low_ref[...], heads_ref, total_ref)

    result = back_close(total_ref, start_ref, mid_ref, norms_ref, out_ref, more_ref)
    send_ref[...] = spread(result, next_gate_ref[:, 0:1], next_cells_ref[...], send_ref.shape[0])


class ExpertWeights:
    def __init__(self, layer, flag_ref, own, theirs, held, sems, order):
        self.own, self.held, self.sems = own, held, sems
        here = flag_ref[0] == layer

        def fetch(sources):
            for expert in range(sources[0].shape[0]):
                for k in order:
                    pltpu.make_async_copy(
                        sources[k].at[expert], held[k].at[expert], sems.at[2 * expert + k]
                    ).start()

        @pl.when(here)
        def _():
            fetch(own)

        @pl.when(jnp.logical_not(here))
        def _():
            fetch(theirs)

    def take(self, expert, k):
        pltpu.make_async_copy(
            self.own[k].at[expert], self.held[k].at[expert], self.sems.at[2 * expert + k]
        ).wait()
        return self.held[k][expert]


def share_out(outer, expert, out_refs):
    size = outer.shape[0] // len(out_refs)
    for d, out_ref in enumerate(out_refs):
        out_ref[expert] = outer[d * size : (d + 1) * size]


def expert_kernel(layer, tensors, flag_ref, *refs):
    row_refs, refs = refs[:tensors], refs[tensors:]
    own, theirs, refs = refs[:2], refs[2:4], refs[4:]
    out_refs, (packed_ref, hidden_ref, slope_ref, *held, sems) = refs[:tensors], refs[tensors:]
    weights = ExpertWeights(layer, flag_ref, own, theirs, held, sems, (0, 1))

    @pl.loop(0, packed_ref.shape[0])
    def _(expert):
        rows = jnp.concatenate([ref[expert] for ref in row_refs], axis=0)
        packed_ref[expert] = rows
        inner = dot(rows, weights.take(expert, 0))
        hidden = gelu_value(inner).astype(bf16)
        hidden_ref[expert] = hidden
        slope_ref[expert] = gelu_slope(inner).astype(bf16)
        share_out(dot(hidden, weights.take(expert, 1)).astype(bf16), expert, out_refs)


def expert_back_kernel(layer, tensors, flag_ref, *refs):
    row_refs, refs = refs[:tensors], refs[tensors:]
    slope_ref = refs[0]
    own, theirs, refs = refs[1:3], refs[3:5], refs[5:]
    out_refs, (packed_ref, inner_ref, *held, sems) = refs[:tensors], refs[tensors:]
    weights = ExpertWeights(layer, flag_ref, own, theirs, held, sems, (1, 0))

    @pl.loop(0, packed_ref.shape[0])
    def _(expert):
        rows = jnp.concatenate([ref[expert] for ref in row_refs], axis=0)
        packed_ref[expert] = rows
        slope = slope_ref[expert].astype(f32)
        inner_grad = (dot_nt(rows, weights.take(expert, 1)) * slope).astype(bf16)
        inner_ref[expert] = inner_grad
        share_out(dot_nt(inner_grad, weights.take(expert, 0)).astype(bf16), expert, out_refs)


def shaped(shape, dtype):
    return jax.ShapeDtypeStruct(shape, dtype)


def cost_of(flops, byte_count):
    return pl.CostEstimate(flops=flops, bytes_accessed=byte_count, transcendentals=0)


LIMIT = 48 * 1024 * 1024
IN_VMEM = pl.BlockSpec(memory_space=pltpu.VMEM)
IN_SMEM = pl.BlockSpec(memory_space=pltpu.SMEM)
ANYWHERE = pl.BlockSpec(memory_space=pl.ANY)


def run_kernel(kernel, args, kinds, outs, scratch=(), cost=None):
    return pl.pallas_call(
        kernel,
        in_specs=[kinds.get(i, IN_VMEM) for i in range(len(args))],
        out_specs=[IN_VMEM] * len(outs),
        out_shape=outs,
        scratch_shapes=list(scratch),
        cost_estimate=cost,
        compiler_params=pltpu.CompilerParams(vmem_limit_bytes=LIMIT),
    )(*args)


def weight_scratch(weights, blocks, tensors):
    rows, features = weights[0].shape
    return [
        pltpu.VMEM((blocks, rows, features), bf16),
        pltpu.SemaphoreType.DMA((4 * tensors,)),
    ]


def front(layer, flag, start, tables, norms, router, picks, cells_row, weights, share):
    joined = start is not None
    tensors = len(tables)
    length = picks.shape[0]
    rows, features = weights[0].shape
    rows_low = shaped((length, features), bf16)
    outs = [rows_low, rows_low] if joined else []
    outs = outs + [
        rows_low,
        shaped((tensors, 4, length, rows // 4), bf16),
        shaped((length, features), f32),
        rows_low,
        shaped((length, 128), f32),
        shaped((share, features), bf16),
    ]
    args = [flag] + list(start or ()) + list(tables) + [norms, router, picks, cells_row]
    kinds = {0: IN_SMEM}
    kinds.update({len(args) + i: ANYWHERE for i in range(len(weights))})
    return run_kernel(
        functools.partial(front_kernel, layer, joined, tensors, len(weights)),
        args + list(weights),
        kinds,
        outs,
        weight_scratch(weights, tensors, tensors),
        cost_of(3_000_000_000, 9_000_000),
    )


def join(middle, gate, cells, tables):
    rows_low = shaped(middle.shape, bf16)
    return run_kernel(
        combine_kernel, [middle, gate, cells] + list(tables), {}, [rows_low, rows_low],
        cost=cost_of(800_000_000, 3_000_000),
    )


def spread_rows(gate, cells_row, grads, share):
    length = gate.shape[0]
    features = grads[0].shape[1]
    outs = [shaped((length, features), bf16), shaped((share, features), bf16)]
    return run_kernel(
        spread_kernel, [gate, cells_row] + list(grads), {}, outs, cost=cost_of(100_000_000, 1_000_000)
    )


def back_first(layer, openers, tables, weights):
    length, features = openers[1].shape
    tensors = len(tables)
    width = openers[10].shape[3]
    experts = openers[6].shape[0]
    args = list(openers) + list(tables)
    kinds = {0: IN_SMEM}
    kinds.update({len(args) + i: ANYWHERE for i in range(len(weights))})
    wide = shaped((length, features), f32)
    outs = [
        shaped((3, length, width), bf16),
        shaped((length, features), bf16),
        shaped((8 + experts, features), f32),
        wide,
        wide,
    ]
    return run_kernel(
        functools.partial(back_first_kernel, layer, tensors, len(weights)),
        args + list(weights),
        kinds,
        outs,
        weight_scratch(weights, 1, tensors),
        cost_of(2_000_000_000, 6_000_000),
    )


def back_rest(layer, flag, low, mid, total, norms, start, heads, weights):
    length, features = low.shape
    tensors = heads.shape[0]
    args = [flag, low, mid, total, norms, start, heads]
    kinds = {0: IN_SMEM}
    kinds.update({len(args) + i: ANYWHERE for i in range(len(weights))})
    return run_kernel(
        functools.partial(back_rest_kernel, layer, tensors, len(weights)),
        args + list(weights),
        kinds,
        [shaped((length, features), bf16), shaped((8, features), f32)],
        [pltpu.VMEM((length, features), f32)] + weight_scratch(weights, tensors - 1, tensors),
        cost_of(4_000_000_000, 9_000_000),
    )


def back(layer, openers, tables, start, weights, next_gate, next_cells, share):
    length, features = openers[1].shape
    tensors = len(tables)
    width = openers[10].shape[3]
    experts = openers[6].shape[0]
    args = list(openers) + list(tables) + [start]
    kinds = {0: IN_SMEM}
    kinds.update({len(args) + i: ANYWHERE for i in range(len(weights))})
    args = args + list(weights) + [next_gate, next_cells]
    rows_low = shaped((length, features), bf16)
    wide = pltpu.VMEM((length, features), f32)
    return run_kernel(
        functools.partial(back_kernel, layer, tensors, len(weights)),
        args,
        kinds,
        [
            shaped((3, length, width), bf16),
            rows_low,
            shaped((8 + experts, features), f32),
            rows_low,
            shaped((8, features), f32),
            shaped((share, features), bf16),
        ],
        [wide, wide] + weight_scratch(weights, tensors, tensors),
        cost_of(5_000_000_000, 12_000_000),
    )


def run_experts(kernel, layer, flag, rows, more, own, theirs, extra):
    args = [flag] + list(rows) + list(more)
    kinds = {0: IN_SMEM}
    kinds.update({len(args) + i: ANYWHERE for i in range(4)})
    return run_kernel(
        functools.partial(kernel, layer, len(rows)),
        args + list(own) + list(theirs),
        kinds,
        [shaped(r.shape, bf16) for r in rows] + list(extra),
        [pltpu.VMEM(w.shape, bf16) for w in own]
        + [pltpu.SemaphoreType.DMA((2 * own[0].shape[0],))],
        cost_of(1_200_000_000, 9_000_000),
    )


def per_device(
    tokens,
    cotangent,
    norm_gains,
    norm_shifts,
    w_qkv,
    w_attn_out,
    w_router,
    w_in,
    w_out,
    choices,
    slot_ranks,
):
    section = lax.axis_index("section")
    tensor = lax.axis_index("tensor")
    here = lax.axis_index("expert")
    tensors = lax.axis_size("tensor")
    owners = lax.axis_size("expert")
    features = tokens.shape[3]
    own_rows = tokens.shape[2]
    length = choices.shape[3]
    experts = w_router.shape[2]
    local = w_in.shape[1]
    hidden_count = w_in.shape[3]
    capacity = 2 * length // experts
    part = capacity // tensors
    share = experts * part
    on_first = section == 0
    flag = section.astype(jnp.int32).reshape(1)

    def swap(block):
        return flip(block, "section", 1)

    def both_layers(block):
        theirs = swap(block)
        return [jnp.where(section == layer, block, theirs) for layer in range(2)]

    def by_core(first, second):
        return jnp.where(on_first, first, second)

    own_weight = jnp.concatenate(
        [
            jnp.transpose(w_qkv[0], (0, 2, 3, 1)).reshape(-1, features),
            w_attn_out[0].reshape(-1, features),
        ]
    )
    swapped_weight = swap(own_weight)
    half = own_weight.shape[0] // 2

    def all_heads(layer):
        if layer == 0:
            piece = by_core(own_weight[:half], swapped_weight[half:])
        else:
            piece = by_core(swapped_weight[:half], own_weight[half:])
        one, two = piece[: half // 2], piece[half // 2 :]
        one_x, two_y = flip(one, "tensor", 1), flip(two, "tensor", 2)
        one_y, two_x = flip(one, "tensor", 2), flip(two, "tensor", 1)
        one_far, two_far = flip(one_x, "tensor", 2), flip(two_y, "tensor", 1)
        mine = [one_x, two_x, one_y, two_y, one_far, two_far]
        return [own_weight, swapped_weight] + mine + [swap(block) for block in mine]

    weights = [all_heads(0), all_heads(1)]
    rows = gather_tensor(by_core(tokens[0, 0], tokens[1, 0]))

    order = jnp.arange(tensors) ^ tensor
    table = jnp.stack([choices[0, :, 0], slot_ranks[0, :, 0]], axis=1)
    table = jnp.swapaxes(table, 2, 3)
    mine = by_core(table[0], table[1])
    theirs = swap(by_core(table[1], table[0]))
    picks, cells, cells_row = [], [], []
    for layer in range(2):
        route = jnp.where(section == layer, mine, theirs)
        route = route.reshape(2, 2, tensors, own_rows)[:, :, order].reshape(2, 2, length)
        pick, slot = route[0], route[1]
        owner = (pick // local - here) % owners
        block = (slot // part) ^ tensor
        cell = block * share + (owner * local + pick % local) * part + slot % part
        cell = jnp.where(slot < capacity, cell, tensors * share)
        picks.append(pick.T)
        cells.append(cell.T)
        cells_row.append(cell)

    norms = both_layers(jnp.concatenate([norm_gains[0], norm_shifts[0]]))
    router = both_layers(w_router[0].T)
    own_experts = (w_in[0], w_out[0])
    their_experts = (swap(w_in[0]), swap(w_out[0]))

    def send_out(sent):
        arrived = to_owners(list(sent.reshape(owners, local, part, features)))
        return gather_tensor(jnp.concatenate(arrived, axis=1))

    def bring_back(parts):
        came = exchange_tensor(parts)
        total = came[0].astype(f32)
        for one in came[1:]:
            total = total + one.astype(f32)
        total = total.astype(bf16)
        blocks = [total[:, s * part : (s + 1) * part].reshape(-1, features) for s in range(owners)]
        return gather_tensor(jnp.concatenate(from_owners(blocks)))

    packed = shaped((local, tensors * owners * part, features), bf16)
    packed_hidden = shaped((local, tensors * owners * part, hidden_count), bf16)
    kept = []
    start, tables = None, rows
    for layer in range(2):
        made = front(
            layer, flag, start, tables, norms[layer], router[layer], picks[layer], cells_row[layer],
            weights[layer], share,
        )
        if layer:
            kept[0]["result"], kept[0]["gap"] = made[:2]
            base = made[0]
            made = made[2:]
        else:
            base = jnp.concatenate(rows)
        normed, heads, middle, second, gate, sent = made
        arrived = send_out(sent)
        done = run_experts(
            expert_kernel, layer, flag, arrived, (), own_experts, their_experts,
            (packed, packed_hidden, packed_hidden),
        )
        tables = bring_back(done[:tensors])
        start = (middle, gate, cells[layer])
        kept.append(
            dict(
                rows=base, normed=normed, heads=heads, middle=middle, second=second, gate=gate,
                arrived=done[tensors], hidden=done[tensors + 1], slope=done[tensors + 2],
            )
        )
    kept[1]["result"], kept[1]["gap"] = join(*start, tables)

    def to_layer_owner(first_layer, second_layer):
        return by_core(first_layer, second_layer), swap(by_core(second_layer, first_layer))

    def by_micro(first_layer, second_layer):
        mine, theirs = to_layer_owner(first_layer, second_layer)
        return jnp.stack([by_core(mine, theirs), by_core(theirs, mine)])

    section_out = by_micro(kept[0]["result"][:own_rows], kept[1]["result"][:own_rows])

    def images_begin(block):
        size = block.shape[0] // 2
        mine = by_core(block[:size], block[size:])
        theirs = swap(by_core(block[size:], block[:size]))
        total = (mine.astype(f32) + theirs.astype(f32)).astype(bf16)
        return total.reshape(owners, -1, features)

    def images_sum(parts):
        total = lax.dynamic_index_in_dim(parts, here, 0, keepdims=False).astype(f32)
        for d in range(1, owners):
            piece = lax.dynamic_index_in_dim(parts, (here + d) % owners, 0, keepdims=False)
            came = rotate(piece, "expert", d)
            total = total + came.astype(f32)
        return total.astype(bf16)

    def images_end(total):
        others = [rotate(total, "expert", -d) for d in range(1, owners)]
        held = jnp.stack([total] + others)
        return jnp.roll(held, here, axis=0).reshape(-1, features)

    def sum_small(first_layer, second_layer):
        small = by_core(first_layer, second_layer) + swap(by_core(second_layer, first_layer))
        step = 1
        while step < owners:
            came = flip(small, "expert", step)
            small = small + came
            step *= 2
        return small

    def dense_of(kept_layer, own_grad, low):
        pieces = [dot_tn(own_grad[member], kept_layer["normed"]) for member in range(3)]
        pieces.append(dot_tn(kept_layer["heads"][0, 3], low))
        return jnp.concatenate([piece.astype(bf16) for piece in pieces])

    gathered = gather_tensor(by_core(cotangent[0, 0], cotangent[1, 0]).astype(bf16))
    grad, sent = spread_rows(kept[1]["gate"], cells_row[1], gathered, share)
    grads, smalls, denses, backs, inner_grads = [None] * 2, [None] * 2, [None] * 2, [None] * 2, [None] * 2
    for layer in (1, 0):
        k = kept[layer]
        came = send_out(sent)
        done = run_experts(
            expert_back_kernel, layer, flag, came, (k["slope"],), own_experts, their_experts,
            (packed, packed_hidden),
        )
        backs[layer], inner_grads[layer] = done[tensors:]
        tables = bring_back(done[:tensors])
        openers = [
            flag, grad, k["gap"], k["gate"], picks[layer], cells[layer], router[layer], norms[layer],
            k["middle"], k["second"], k["heads"],
        ]
        if layer:
            own_grad, low, small, grad, more, sent = back(
                layer, openers, tables, k["rows"], weights[layer], kept[0]["gate"], cells_row[0], share
            )
        else:
            own_grad, low, small, mid, total = back_first(layer, openers, tables, weights[layer])
            grad, more = back_rest(
                layer, flag, low, mid, total, norms[layer], k["rows"], k["heads"], weights[layer]
            )
        grads[layer] = grad
        smalls[layer] = jnp.concatenate([small[:8] + more, small[8:]])
        denses[layer] = images_sum(images_begin(dense_of(k, own_grad, low)))
    denses = [images_end(total) for total in denses]
    input_grad = by_micro(grads[0][:own_rows], grads[1][:own_rows])
    small = sum_small(*smalls)
    mine, theirs = to_layer_owner(denses[0], denses[1])
    dense = jnp.concatenate([by_core(mine, theirs), by_core(theirs, mine)]).astype(f32)
    dense = dense.reshape(4, -1, features)

    def weight_grad(lefts, rights):
        left_own, left_their = to_layer_owner(*lefts)
        right_own, right_their = to_layer_owner(*rights)
        spec = "jrd,jrf->jdf"
        return jnp.einsum(spec, left_own, right_own, preferred_element_type=f32) + jnp.einsum(
            spec, left_their, right_their, preferred_element_type=f32
        )

    grad_first = weight_grad([k["arrived"] for k in kept], inner_grads)
    grad_second = weight_grad([k["hidden"] for k in kept], backs)
    qkv_grad = dense[:3].reshape(3, -1, HEAD_DIM, features)
    return (
        section_out[None, :, None],
        input_grad[None, :, None],
        small[0:2][None],
        small[2:4][None],
        jnp.transpose(qkv_grad, (0, 3, 1, 2))[None],
        dense[3].reshape(w_attn_out.shape),
        small[8 : 8 + experts].T[None],
        grad_first[None],
        grad_second[None],
    )


def solution(mesh):
    return jax.shard_map(
        per_device,
        mesh=mesh,
        in_specs=(
            P(None, "expert", "tensor", None),
            P(None, "expert", "tensor", None),
            P("section", None, None),
            P("section", None, None),
            P("section", None, None, "tensor", None),
            P("section", "tensor", None, None),
            P("section", None, None),
            P("section", "expert", None, "tensor"),
            P("section", "expert", "tensor", None),
            P("section", None, "expert", None, None),
            P("section", None, "expert", None, None),
        ),
        out_specs=(
            P("section", None, "expert", "tensor", None),
            P("section", None, "expert", "tensor", None),
            P("section", None, None),
            P("section", None, None),
            P("section", None, None, "tensor", None),
            P("section", "tensor", None, None),
            P("section", None, None),
            P("section", "expert", None, "tensor"),
            P("section", "expert", "tensor", None),
        ),
        check_vma=False,
    )
```

```python
import functools

import jax
import jax.numpy as jnp
from jax import lax
from jax.experimental import pallas as pl
from jax.experimental.pallas import tpu as pltpu
from jax.sharding import PartitionSpec as P


HEAD_DIM = 64
HEAD_SCALE = 0.125

norm_eps = 1e-06
half_root = 0.7071067811865476
tau_root = 0.3989422804014327
bf16 = jnp.bfloat16
f32 = jnp.float32


def gelu_value(values):
    return 0.5 * values * (1.0 + lax.erf(values * half_root))


def gelu_slope(values):
    return (
        0.5 * (1.0 + lax.erf(values * half_root))
        + values * jnp.exp(-0.5 * values * values) * tau_root
    )


def unit_of(values):
    center = jnp.mean(values, axis=-1, keepdims=True)
    deviation = values - center
    factor = lax.rsqrt(jnp.mean(deviation * deviation, axis=-1, keepdims=True) + norm_eps)
    return deviation * factor, factor


def norm_back(grad_norm, unit_rows, factor, gain_row):
    scaled = grad_norm * gain_row
    return factor * (
        scaled
        - jnp.mean(scaled, axis=-1, keepdims=True)
        - unit_rows * jnp.mean(scaled * unit_rows, axis=-1, keepdims=True)
    )


def dot(left, right):
    return jnp.dot(left, right, preferred_element_type=f32)


def dot_tn(left, right):
    return lax.dot_general(left, right, (((0,), (0,)), ((), ())), preferred_element_type=f32)


def dot_nt(left, right):
    return lax.dot_general(left, right, (((1,), (1,)), ((), ())), preferred_element_type=f32)


def flip(block, axis, mask):
    return lax.ppermute(block, axis, [(i, i ^ mask) for i in range(lax.axis_size(axis))])


def rotate(block, axis, distance):
    count = lax.axis_size(axis)
    return lax.ppermute(block, axis, [(i, (i + distance) % count) for i in range(count)])


def gather_tensor(own):
    return [own] + [flip(own, "tensor", d) for d in range(1, lax.axis_size("tensor"))]


def exchange_tensor(parts):
    return [parts[0]] + [flip(parts[d], "tensor", d) for d in range(1, len(parts))]


def to_owners(blocks):
    return [blocks[0]] + [rotate(blocks[d], "expert", d) for d in range(1, len(blocks))]


def from_owners(blocks):
    return [blocks[0]] + [rotate(blocks[d], "expert", -d) for d in range(1, len(blocks))]


def joined_rows(refs):
    return jnp.concatenate([ref[...] for ref in refs], axis=0)


def lane_mask(head, width):
    lanes = lax.broadcasted_iota(jnp.int32, (1, width), 1)
    return (lanes // HEAD_DIM == head).astype(bf16)


def stack_heads(rows):
    width = rows.shape[1]
    return jnp.concatenate([rows * lane_mask(h, width) for h in range(width // HEAD_DIM)], axis=0)


def fold_heads(stacked):
    width = stacked.shape[1]
    count = width // HEAD_DIM
    size = stacked.shape[0] // count
    total = stacked[:size]
    lanes = lax.broadcasted_iota(jnp.int32, (1, width), 1) // HEAD_DIM
    for head in range(1, count):
        total = jnp.where(lanes == head, stacked[head * size : (head + 1) * size], total)
    return total


def pick_rows(cell_column, count):
    ids = lax.broadcasted_iota(jnp.int32, (cell_column.shape[0], count), 1)
    return ids == cell_column


def pick_cells(cell_row, count):
    ids = lax.broadcasted_iota(jnp.int32, (count, cell_row.shape[1]), 0)
    return ids == cell_row


def expert_sign(pick_column, experts):
    ids = lax.broadcasted_iota(jnp.int32, (pick_column.shape[0], experts), 1)
    return (ids == pick_column).astype(f32)


def combine(middle, gate, cells, table):
    count = table.shape[0]
    first = dot(pick_rows(cells[:, 0:1], count).astype(bf16), table)
    second = dot(pick_rows(cells[:, 1:2], count).astype(bf16), table)
    return middle + gate * first + (1.0 - gate) * second, first - second


def combine_kernel(middle_ref, gate_ref, cells_ref, *refs):
    result_ref, gap_ref = refs[-2:]
    total, gap = combine(
        middle_ref[...], gate_ref[:, 0:1], cells_ref[...], joined_rows(refs[:-2])
    )
    result_ref[...] = total.astype(bf16)
    gap_ref[...] = gap.astype(bf16)


class Weights:
    def __init__(self, layer, flag_ref, refs, held_ref, sems, blocks):
        own, swapped = refs[:2]
        pieces = (len(refs) - 2) // 2
        mine, theirs = refs[2 : 2 + pieces], refs[2 + pieces :]
        width = held_ref.shape[1] // 4
        self.held, self.sems, self.width = held_ref, sems, width
        self.piece = mine[0]
        self.first = blocks[0]
        on_first = flag_ref[0] == 0
        here = flag_ref[0] == layer

        def fetch(source, block, k):
            place = held_ref.at[block - self.first, pl.ds(k * width, width)]
            pltpu.make_async_copy(source, place, sems.at[4 * block + k]).start()

        def fetch_own(source):
            for k in range(4):
                fetch(source.at[pl.ds(k * width, width)], 0, k)

        def fetch_all(low, high):
            for block in blocks:
                for k in range(2 if block else 0):
                    index = 2 * (block - 1) + k
                    fetch(low[index], block, k)
                    fetch(high[index], block, k + 2)

        if 0 in blocks:

            @pl.when(here)
            def _():
                fetch_own(own)

            @pl.when(jnp.logical_not(here))
            def _():
                fetch_own(swapped)

        @pl.when(on_first)
        def _():
            fetch_all(mine, theirs)

        @pl.when(jnp.logical_not(on_first))
        def _():
            fetch_all(theirs, mine)

    def wait(self, block):
        for k in range(4):
            place = self.held.at[block - self.first, pl.ds(k * self.width, self.width)]
            pltpu.make_async_copy(self.piece, place, self.sems.at[4 * block + k]).wait()

    def member(self, block, index):
        return self.held[block - self.first, pl.ds(index * self.width, self.width)]


def front_kernel(layer, joined, tensors, weight_count, *refs):
    refs = list(refs)
    flag_ref = refs.pop(0)
    if joined:
        before_ref, before_gate_ref, before_cells_ref = refs[:3]
        refs = refs[3:]
    table_refs, refs = refs[:tensors], refs[tensors:]
    norms_ref, router_ref, picks_ref, cells_ref = refs[:4]
    weight_refs, refs = refs[4 : 4 + weight_count], refs[4 + weight_count :]
    if joined:
        result_ref, gap_ref = refs[:2]
        refs = refs[2:]
    normed_ref, heads_ref, middle_ref, second_ref, gate_ref, send_ref, held_ref, sems = refs
    weights = Weights(layer, flag_ref, weight_refs, held_ref, sems, range(tensors))
    if joined:
        total, gap = combine(
            before_ref[...], before_gate_ref[:, 0:1], before_cells_ref[...], joined_rows(table_refs)
        )
        low = total.astype(bf16)
        result_ref[...] = low
        gap_ref[...] = gap.astype(bf16)
    else:
        low = joined_rows(table_refs)
    start = low.astype(f32)
    unit, _ = unit_of(start)
    normed_ref[...] = (unit * norms_ref[0:1] + norms_ref[2:3]).astype(bf16)
    middle_ref[...] = start

    def heads_of(block):
        weights.wait(block)
        normed = normed_ref[...]
        query = dot_nt(normed, weights.member(block, 0)).astype(bf16)
        key = dot_nt(normed, weights.member(block, 1)).astype(bf16)
        value = dot_nt(normed, weights.member(block, 2)).astype(bf16)
        scores = dot_nt(stack_heads(query * HEAD_SCALE), key)
        soft = jnp.exp(scores - jnp.log(jnp.sum(jnp.exp(scores), axis=-1, keepdims=True)))
        attended = fold_heads(dot(soft.astype(bf16), value)).astype(bf16)
        heads_ref[block, 0] = query
        heads_ref[block, 1] = key
        heads_ref[block, 2] = value
        heads_ref[block, 3] = attended
        middle_ref[...] += dot(attended, weights.member(block, 3))

    heads_of(0)

    @pl.loop(1, tensors)
    def _(block):
        heads_of(block)

    unit, _ = unit_of(middle_ref[...])
    second = (unit * norms_ref[1:2] + norms_ref[3:4]).astype(bf16)
    second_ref[...] = second
    logits = dot_nt(second, router_ref[...])
    experts = logits.shape[1]
    sign = expert_sign(picks_ref[:, 0:1], experts) - expert_sign(picks_ref[:, 1:2], experts)
    gap = jnp.sum(sign * logits, axis=-1, keepdims=True)
    gate = 1.0 / (1.0 + jnp.exp(-gap))
    gate_ref[...] = jnp.broadcast_to(gate, gate_ref.shape)
    count = send_ref.shape[0]
    hit = pick_cells(cells_ref[0:1], count) | pick_cells(cells_ref[1:2], count)
    send_ref[...] = dot(hit.astype(bf16), second).astype(bf16)


def spread(grad, gate, cells_row, count):
    wide = grad.astype(f32)
    first = (wide * gate).astype(bf16)
    second = (wide * (1.0 - gate)).astype(bf16)
    total = dot(pick_cells(cells_row[0:1], count).astype(bf16), first)
    total = total + dot(pick_cells(cells_row[1:2], count).astype(bf16), second)
    return total.astype(bf16)


def spread_kernel(gate_ref, cells_ref, *refs):
    grad_refs, (grad_ref, send_ref) = refs[:-2], refs[-2:]
    grad = joined_rows(grad_refs)
    grad_ref[...] = grad
    send_ref[...] = spread(grad, gate_ref[:, 0:1], cells_ref[...], send_ref.shape[0])


def back_heads(weights, block, low, heads_ref, total_ref):
    weights.wait(block)
    out_grad = dot_nt(low, weights.member(block, 3)).astype(bf16)
    query = heads_ref[block, 0]
    key = heads_ref[block, 1]
    value = heads_ref[block, 2]
    count = query.shape[1] // HEAD_DIM
    length = query.shape[0]

    def by_head(stacked):
        return stacked.reshape(count, length, length)

    scaled = query * HEAD_SCALE
    own_keys = stack_heads(key)
    scores = by_head(dot_nt(own_keys, scaled))
    probs = jnp.exp(scores - jnp.log(jnp.sum(jnp.exp(scores), axis=1, keepdims=True)))
    prob_grad = by_head(dot_nt(stack_heads(value), out_grad))
    row_dot = jnp.sum(probs * prob_grad, axis=1, keepdims=True)
    score_grad = (probs * (prob_grad - row_dot)).astype(bf16).reshape(count * length, length)
    value_grad = fold_heads(dot(probs.astype(bf16).reshape(count * length, length), out_grad))
    key_grad = fold_heads(dot(score_grad, scaled))
    query_grad = dot_tn(score_grad, own_keys) * HEAD_SCALE
    made = (query_grad.astype(bf16), key_grad.astype(bf16), value_grad.astype(bf16))
    part = dot(made[0], weights.member(block, 0))
    part = part + dot(made[1], weights.member(block, 1)) + dot(made[2], weights.member(block, 2))
    if isinstance(block, int):
        total_ref[...] = part
    else:
        total_ref[...] += part
    return made


def back_open(openers, table_refs, low_ref, small_ref, mid_ref):
    (
        _,
        grad_ref,
        gap_ref,
        gate_ref,
        picks_ref,
        cells_ref,
        router_ref,
        norms_ref,
        middle_ref,
        second_ref,
        _,
    ) = openers
    experts = router_ref.shape[0]
    grad = grad_ref[...].astype(f32)
    gate = gate_ref[:, 0:1]
    change = jnp.sum(grad * gap_ref[...].astype(f32), axis=-1, keepdims=True)
    sign = expert_sign(picks_ref[:, 0:1], experts) - expert_sign(picks_ref[:, 1:2], experts)
    logit_grad = (gate * (1.0 - gate) * change * sign).astype(bf16)
    table = joined_rows(table_refs)
    count = table.shape[0]
    hit = pick_rows(cells_ref[:, 0:1], count) | pick_rows(cells_ref[:, 1:2], count)
    normed_grad = dot(hit.astype(bf16), table) + dot(logit_grad, router_ref[...])
    unit, factor = unit_of(middle_ref[...])
    mid = grad + norm_back(normed_grad, unit, factor, norms_ref[1:2])
    small_ref[...] = jnp.zeros_like(small_ref)
    small_ref[1:2] = jnp.sum(normed_grad * unit, axis=0, keepdims=True)
    small_ref[3:4] = jnp.sum(normed_grad, axis=0, keepdims=True)
    small_ref[8 : 8 + experts] = dot_tn(logit_grad, second_ref[...])
    mid_ref[...] = mid
    low = mid.astype(bf16)
    low_ref[...] = low


def keep_own(own_ref, made):
    for index in range(3):
        own_ref[index] = made[index]


def back_close(total_ref, start_ref, mid_ref, norms_ref, out_ref, small_ref):
    first_grad = total_ref[...]
    unit, factor = unit_of(start_ref[...].astype(f32))
    small_ref[...] = jnp.zeros_like(small_ref)
    small_ref[0:1] = jnp.sum(first_grad * unit, axis=0, keepdims=True)
    small_ref[2:3] = jnp.sum(first_grad, axis=0, keepdims=True)
    result = (mid_ref[...] + norm_back(first_grad, unit, factor, norms_ref[0:1])).astype(bf16)
    out_ref[...] = result
    return result


def back_first_kernel(layer, tensors, weight_count, *refs):
    refs = list(refs)
    openers, refs = refs[:11], refs[11:]
    table_refs, refs = refs[:tensors], refs[tensors:]
    weight_refs, refs = refs[:weight_count], refs[weight_count:]
    own_ref, low_ref, small_ref, mid_ref, total_ref, held_ref, sems = refs
    weights = Weights(layer, openers[0], weight_refs, held_ref, sems, [0])
    back_open(openers, table_refs, low_ref, small_ref, mid_ref)
    keep_own(own_ref, back_heads(weights, 0, low_ref[...], openers[10], total_ref))


def back_rest_kernel(layer, tensors, weight_count, *refs):
    refs = list(refs)
    flag_ref, low_ref, mid_ref, before_ref, norms_ref, start_ref, heads_ref = refs[:7]
    refs = refs[7:]
    weight_refs, refs = refs[:weight_count], refs[weight_count:]
    out_ref, small_ref, total_ref, held_ref, sems = refs
    weights = Weights(layer, flag_ref, weight_refs, held_ref, sems, range(1, tensors))
    total_ref[...] = before_ref[...]

    @pl.loop(1, tensors)
    def _(block):
        back_heads(weights, block, low_ref[...], heads_ref, total_ref)

    back_close(total_ref, start_ref, mid_ref, norms_ref, out_ref, small_ref)


def back_kernel(layer, tensors, weight_count, *refs):
    refs = list(refs)
    openers, refs = refs[:11], refs[11:]
    table_refs, refs = refs[:tensors], refs[tensors:]
    start_ref, refs = refs[0], refs[1:]
    weight_refs, refs = refs[:weight_count], refs[weight_count:]
    next_gate_ref, next_cells_ref = refs[:2]
    own_ref, low_ref, small_ref, out_ref, more_ref, send_ref, mid_ref, total_ref, held_ref, sems = refs[2:]
    norms_ref, heads_ref = openers[7], openers[10]
    weights = Weights(layer, openers[0], weight_refs, held_ref, sems, range(tensors))
    back_open(openers, table_refs, low_ref, small_ref, mid_ref)

    keep_own(own_ref, back_heads(weights, 0, low_ref[...], heads_ref, total_ref))

    @pl.loop(1, tensors)
    def _(block):
        back_heads(weights, block, low_ref[...], heads_ref, total_ref)

    result = back_close(total_ref, start_ref, mid_ref, norms_ref, out_ref, more_ref)
    send_ref[...] = spread(result, next_gate_ref[:, 0:1], next_cells_ref[...], send_ref.shape[0])


def back_kernel(layer, tensors, weight_count, *refs):
    refs = list(refs)
    openers, refs = refs[:11], refs[11:]
    table_refs, refs = refs[:tensors], refs[tensors:]
    start_ref, refs = refs[0], refs[1:]
    weight_refs, refs = refs[:weight_count], refs[weight_count:]
    next_gate_ref, next_cells_ref = refs[:2]
    own_ref, low_ref, small_ref, out_ref, more_ref, send_ref, mid_ref, total_ref, held_ref, sems = refs[2:]
    norms_ref, heads_ref = openers[7], openers[10]
    weights = Weights(layer, openers[0], weight_refs, held_ref, sems, range(tensors))
    back_open(openers, table_refs, low_ref, small_ref, mid_ref)

    keep_own(own_ref, back_heads(weights, 0, low_ref[...], heads_ref, total_ref))

    @pl.loop(1, tensors)
    def _(block):
        back_heads(weights, block, low_ref[...], heads_ref, total_ref)

    result = back_close(total_ref, start_ref, mid_ref, norms_ref, out_ref, more_ref)
    send_ref[...] = spread(result, next_gate_ref[:, 0:1], next_cells_ref[...], send_ref.shape[0])


class ExpertWeights:
    def __init__(self, layer, flag_ref, own, theirs, held, sems, order):
        self.own, self.held, self.sems = own, held, sems
        here = flag_ref[0] == layer

        def fetch(sources):
            for expert in range(sources[0].shape[0]):
                for k in order:
                    pltpu.make_async_copy(
                        sources[k].at[expert], held[k].at[expert], sems.at[2 * expert + k]
                    ).start()

        @pl.when(here)
        def _():
            fetch(own)

        @pl.when(jnp.logical_not(here))
        def _():
            fetch(theirs)

    def take(self, expert, k):
        pltpu.make_async_copy(
            self.own[k].at[expert], self.held[k].at[expert], self.sems.at[2 * expert + k]
        ).wait()
        return self.held[k][expert]


def share_out(outer, expert, out_refs):
    size = outer.shape[0] // len(out_refs)
    for d, out_ref in enumerate(out_refs):
        out_ref[expert] = outer[d * size : (d + 1) * size]


def expert_kernel(layer, tensors, flag_ref, *refs):
    row_refs, refs = refs[:tensors], refs[tensors:]
    own, theirs, refs = refs[:2], refs[2:4], refs[4:]
    out_refs, (packed_ref, hidden_ref, slope_ref, *held, sems) = refs[:tensors], refs[tensors:]
    weights = ExpertWeights(layer, flag_ref, own, theirs, held, sems, (0, 1))

    @pl.loop(0, packed_ref.shape[0])
    def _(expert):
        rows = jnp.concatenate([ref[expert] for ref in row_refs], axis=0)
        packed_ref[expert] = rows
        inner = dot(rows, weights.take(expert, 0))
        hidden = gelu_value(inner).astype(bf16)
        hidden_ref[expert] = hidden
        slope_ref[expert] = gelu_slope(inner).astype(bf16)
        share_out(dot(hidden, weights.take(expert, 1)).astype(bf16), expert, out_refs)


def expert_back_kernel(layer, tensors, flag_ref, *refs):
    row_refs, refs = refs[:tensors], refs[tensors:]
    slope_ref = refs[0]
    own, theirs, refs = refs[1:3], refs[3:5], refs[5:]
    out_refs, (packed_ref, inner_ref, *held, sems) = refs[:tensors], refs[tensors:]
    weights = ExpertWeights(layer, flag_ref, own, theirs, held, sems, (1, 0))

    @pl.loop(0, packed_ref.shape[0])
    def _(expert):
        rows = jnp.concatenate([ref[expert] for ref in row_refs], axis=0)
        packed_ref[expert] = rows
        slope = slope_ref[expert].astype(f32)
        inner_grad = (dot_nt(rows, weights.take(expert, 1)) * slope).astype(bf16)
        inner_ref[expert] = inner_grad
        share_out(dot_nt(inner_grad, weights.take(expert, 0)).astype(bf16), expert, out_refs)


def shaped(shape, dtype):
    return jax.ShapeDtypeStruct(shape, dtype)


def cost_of(flops, byte_count):
    return pl.CostEstimate(flops=flops, bytes_accessed=byte_count, transcendentals=0)


LIMIT = 48 * 1024 * 1024
IN_VMEM = pl.BlockSpec(memory_space=pltpu.VMEM)
IN_SMEM = pl.BlockSpec(memory_space=pltpu.SMEM)
ANYWHERE = pl.BlockSpec(memory_space=pl.ANY)


def run_kernel(kernel, args, kinds, outs, scratch=(), cost=None, limit=LIMIT):
    return pl.pallas_call(
        kernel,
        in_specs=[kinds.get(i, IN_VMEM) for i in range(len(args))],
        out_specs=[IN_VMEM] * len(outs),
        out_shape=outs,
        scratch_shapes=list(scratch),
        cost_estimate=cost,
        compiler_params=pltpu.CompilerParams(vmem_limit_bytes=limit),
    )(*args)


def weight_scratch(weights, blocks, tensors):
    rows, features = weights[0].shape
    return [
        pltpu.VMEM((blocks, rows, features), bf16),
        pltpu.SemaphoreType.DMA((4 * tensors,)),
    ]


def front(layer, flag, start, tables, norms, router, picks, cells_row, weights, share):
    joined = start is not None
    tensors = len(tables)
    length = picks.shape[0]
    rows, features = weights[0].shape
    rows_low = shaped((length, features), bf16)
    outs = [rows_low, rows_low] if joined else []
    outs = outs + [
        rows_low,
        shaped((tensors, 4, length, rows // 4), bf16),
        shaped((length, features), f32),
        rows_low,
        shaped((length, 128), f32),
        shaped((share, features), bf16),
    ]
    args = [flag] + list(start or ()) + list(tables) + [norms, router, picks, cells_row]
    kinds = {0: IN_SMEM}
    kinds.update({len(args) + i: ANYWHERE for i in range(len(weights))})
    return run_kernel(
        functools.partial(front_kernel, layer, joined, tensors, len(weights)),
        args + list(weights),
        kinds,
        outs,
        weight_scratch(weights, tensors, tensors),
        cost_of(3_000_000_000, 9_000_000),
    )


def join(middle, gate, cells, tables):
    rows_low = shaped(middle.shape, bf16)
    return run_kernel(
        combine_kernel, [middle, gate, cells] + list(tables), {}, [rows_low, rows_low],
        cost=cost_of(800_000_000, 3_000_000),
    )


def spread_rows(gate, cells_row, grads, share):
    length = gate.shape[0]
    features = grads[0].shape[1]
    outs = [shaped((length, features), bf16), shaped((share, features), bf16)]
    return run_kernel(
        spread_kernel, [gate, cells_row] + list(grads), {}, outs, cost=cost_of(100_000_000, 1_000_000)
    )


def back_first(layer, openers, tables, weights):
    length, features = openers[1].shape
    tensors = len(tables)
    width = openers[10].shape[3]
    experts = openers[6].shape[0]
    args = list(openers) + list(tables)
    kinds = {0: IN_SMEM}
    kinds.update({len(args) + i: ANYWHERE for i in range(len(weights))})
    wide = shaped((length, features), f32)
    outs = [
        shaped((3, length, width), bf16),
        shaped((length, features), bf16),
        shaped((8 + experts, features), f32),
        wide,
        wide,
    ]
    return run_kernel(
        functools.partial(back_first_kernel, layer, tensors, len(weights)),
        args + list(weights),
        kinds,
        outs,
        weight_scratch(weights, 1, tensors),
        cost_of(2_000_000_000, 6_000_000),
        LIMIT // 2,
    )


def back_rest(layer, flag, low, mid, total, norms, start, heads, weights):
    length, features = low.shape
    tensors = heads.shape[0]
    args = [flag, low, mid, total, norms, start, heads]
    kinds = {0: IN_SMEM}
    kinds.update({len(args) + i: ANYWHERE for i in range(len(weights))})
    return run_kernel(
        functools.partial(back_rest_kernel, layer, tensors, len(weights)),
        args + list(weights),
        kinds,
        [shaped((length, features), bf16), shaped((8, features), f32)],
        [pltpu.VMEM((length, features), f32)] + weight_scratch(weights, tensors - 1, tensors),
        cost_of(4_000_000_000, 9_000_000),
        LIMIT // 2,
    )


def back(layer, openers, tables, start, weights, next_gate, next_cells, share):
    length, features = openers[1].shape
    tensors = len(tables)
    width = openers[10].shape[3]
    experts = openers[6].shape[0]
    args = list(openers) + list(tables) + [start]
    kinds = {0: IN_SMEM}
    kinds.update({len(args) + i: ANYWHERE for i in range(len(weights))})
    args = args + list(weights) + [next_gate, next_cells]
    rows_low = shaped((length, features), bf16)
    wide = pltpu.VMEM((length, features), f32)
    return run_kernel(
        functools.partial(back_kernel, layer, tensors, len(weights)),
        args,
        kinds,
        [
            shaped((3, length, width), bf16),
            rows_low,
            shaped((8 + experts, features), f32),
            rows_low,
            shaped((8, features), f32),
            shaped((share, features), bf16),
        ],
        [wide, wide] + weight_scratch(weights, tensors, tensors),
        cost_of(5_000_000_000, 12_000_000),
    )


def run_experts(kernel, layer, flag, rows, more, own, theirs, extra):
    args = [flag] + list(rows) + list(more)
    kinds = {0: IN_SMEM}
    kinds.update({len(args) + i: ANYWHERE for i in range(4)})
    return run_kernel(
        functools.partial(kernel, layer, len(rows)),
        args + list(own) + list(theirs),
        kinds,
        [shaped(r.shape, bf16) for r in rows] + list(extra),
        [pltpu.VMEM(w.shape, bf16) for w in own]
        + [pltpu.SemaphoreType.DMA((2 * own[0].shape[0],))],
        cost_of(1_200_000_000, 9_000_000),
    )


def per_device(
    tokens,
    cotangent,
    norm_gains,
    norm_shifts,
    w_qkv,
    w_attn_out,
    w_router,
    w_in,
    w_out,
    choices,
    slot_ranks,
):
    section = lax.axis_index("section")
    tensor = lax.axis_index("tensor")
    here = lax.axis_index("expert")
    tensors = lax.axis_size("tensor")
    owners = lax.axis_size("expert")
    features = tokens.shape[3]
    own_rows = tokens.shape[2]
    length = choices.shape[3]
    experts = w_router.shape[2]
    local = w_in.shape[1]
    hidden_count = w_in.shape[3]
    capacity = 2 * length // experts
    part = capacity // tensors
    share = experts * part
    on_first = section == 0
    flag = section.astype(jnp.int32).reshape(1)

    def swap(block):
        return flip(block, "section", 1)

    def both_layers(block):
        theirs = swap(block)
        return [jnp.where(section == layer, block, theirs) for layer in range(2)]

    def by_core(first, second):
        return jnp.where(on_first, first, second)

    own_weight = jnp.concatenate(
        [
            jnp.transpose(w_qkv[0], (0, 2, 3, 1)).reshape(-1, features),
            w_attn_out[0].reshape(-1, features),
        ]
    )
    swapped_weight = swap(own_weight)
    half = own_weight.shape[0] // 2

    def all_heads(layer):
        if layer == 0:
            piece = by_core(own_weight[:half], swapped_weight[half:])
        else:
            piece = by_core(swapped_weight[:half], own_weight[half:])
        one, two = piece[: half // 2], piece[half // 2 :]
        one_x, two_y = flip(one, "tensor", 1), flip(two, "tensor", 2)
        one_y, two_x = flip(one, "tensor", 2), flip(two, "tensor", 1)
        one_far, two_far = flip(one_x, "tensor", 2), flip(two_y, "tensor", 1)
        mine = [one_x, two_x, one_y, two_y, one_far, two_far]
        return [own_weight, swapped_weight] + mine + [swap(block) for block in mine]

    weights = [all_heads(0), all_heads(1)]
    rows = gather_tensor(by_core(tokens[0, 0], tokens[1, 0]))

    order = jnp.arange(tensors) ^ tensor
    table = jnp.stack([choices[0, :, 0], slot_ranks[0, :, 0]], axis=1)
    table = jnp.swapaxes(table, 2, 3)
    mine = by_core(table[0], table[1])
    theirs = swap(by_core(table[1], table[0]))
    picks, cells, cells_row = [], [], []
    for layer in range(2):
        route = jnp.where(section == layer, mine, theirs)
        route = route.reshape(2, 2, tensors, own_rows)[:, :, order].reshape(2, 2, length)
        pick, slot = route[0], route[1]
        owner = (pick // local - here) % owners
        block = (slot // part) ^ tensor
        cell = block * share + (owner * local + pick % local) * part + slot % part
        cell = jnp.where(slot < capacity, cell, tensors * share)
        picks.append(pick.T)
        cells.append(cell.T)
        cells_row.append(cell)

    norms = both_layers(jnp.concatenate([norm_gains[0], norm_shifts[0]]))
    router = both_layers(w_router[0].T)
    own_experts = (w_in[0], w_out[0])
    their_experts = (swap(w_in[0]), swap(w_out[0]))

    def send_out(sent):
        arrived = to_owners(list(sent.reshape(owners, local, part, features)))
        return gather_tensor(jnp.concatenate(arrived, axis=1))

    def bring_back(parts):
        came = exchange_tensor(parts)
        total = came[0].astype(f32)
        for one in came[1:]:
            total = total + one.astype(f32)
        total = total.astype(bf16)
        blocks = [total[:, s * part : (s + 1) * part].reshape(-1, features) for s in range(owners)]
        return gather_tensor(jnp.concatenate(from_owners(blocks)))

    packed = shaped((local, tensors * owners * part, features), bf16)
    packed_hidden = shaped((local, tensors * owners * part, hidden_count), bf16)
    kept = []
    start, tables = None, rows
    for layer in range(2):
        made = front(
            layer, flag, start, tables, norms[layer], router[layer], picks[layer], cells_row[layer],
            weights[layer], share,
        )
        if layer:
            kept[0]["result"], kept[0]["gap"] = made[:2]
            base = made[0]
            made = made[2:]
        else:
            base = jnp.concatenate(rows)
        normed, heads, middle, second, gate, sent = made
        arrived = send_out(sent)
        done = run_experts(
            expert_kernel, layer, flag, arrived, (), own_experts, their_experts,
            (packed, packed_hidden, packed_hidden),
        )
        tables = bring_back(done[:tensors])
        start = (middle, gate, cells[layer])
        kept.append(
            dict(
                rows=base, normed=normed, heads=heads, middle=middle, second=second, gate=gate,
                arrived=done[tensors], hidden=done[tensors + 1], slope=done[tensors + 2],
            )
        )
    kept[1]["result"], kept[1]["gap"] = join(*start, tables)

    def to_layer_owner(first_layer, second_layer):
        return by_core(first_layer, second_layer), swap(by_core(second_layer, first_layer))

    def by_micro(first_layer, second_layer):
        mine, theirs = to_layer_owner(first_layer, second_layer)
        return jnp.stack([by_core(mine, theirs), by_core(theirs, mine)])

    section_out = by_micro(kept[0]["result"][:own_rows], kept[1]["result"][:own_rows])

    def images_begin(block):
        size = block.shape[0] // 2
        mine = by_core(block[:size], block[size:])
        theirs = swap(by_core(block[size:], block[:size]))
        total = (mine.astype(f32) + theirs.astype(f32)).astype(bf16)
        return total.reshape(owners, -1, features)

    def images_sum(parts):
        total = lax.dynamic_index_in_dim(parts, here, 0, keepdims=False).astype(f32)
        for d in range(1, owners):
            piece = lax.dynamic_index_in_dim(parts, (here + d) % owners, 0, keepdims=False)
            came = rotate(piece, "expert", d)
            total = total + came.astype(f32)
        return total.astype(bf16)

    def images_end(total):
        others = [rotate(total, "expert", -d) for d in range(1, owners)]
        held = jnp.stack([total] + others)
        return jnp.roll(held, here, axis=0).reshape(-1, features)

    def sum_small(first_layer, second_layer):
        small = by_core(first_layer, second_layer) + swap(by_core(second_layer, first_layer))
        step = 1
        while step < owners:
            came = flip(small, "expert", step)
            small = small + came
            step *= 2
        return small

    def dense_of(kept_layer, own_grad, low):
        pieces = [dot_tn(own_grad[member], kept_layer["normed"]) for member in range(3)]
        pieces.append(dot_tn(kept_layer["heads"][0, 3], low))
        return jnp.concatenate([piece.astype(bf16) for piece in pieces])

    gathered = gather_tensor(by_core(cotangent[0, 0], cotangent[1, 0]).astype(bf16))
    grad, sent = spread_rows(kept[1]["gate"], cells_row[1], gathered, share)
    grads, smalls, denses, backs, inner_grads = [None] * 2, [None] * 2, [None] * 2, [None] * 2, [None] * 2
    for layer in (1, 0):
        k = kept[layer]
        came = send_out(sent)
        done = run_experts(
            expert_back_kernel, layer, flag, came, (k["slope"],), own_experts, their_experts,
            (packed, packed_hidden),
        )
        backs[layer], inner_grads[layer] = done[tensors:]
        tables = bring_back(done[:tensors])
        openers = [
            flag, grad, k["gap"], k["gate"], picks[layer], cells[layer], router[layer], norms[layer],
            k["middle"], k["second"], k["heads"],
        ]
        if layer:
            own_grad, low, small, grad, more, sent = back(
                layer, openers, tables, k["rows"], weights[layer], kept[0]["gate"], cells_row[0], share
            )
        else:
            own_grad, low, small, mid, total = back_first(layer, openers, tables, weights[layer])
            grad, more = back_rest(
                layer, flag, low, mid, total, norms[layer], k["rows"], k["heads"], weights[layer]
            )
        grads[layer] = grad
        smalls[layer] = jnp.concatenate([small[:8] + more, small[8:]])
        denses[layer] = images_sum(images_begin(dense_of(k, own_grad, low)))
    denses = [images_end(total) for total in denses]
    input_grad = by_micro(grads[0][:own_rows], grads[1][:own_rows])
    small = sum_small(*smalls)
    mine, theirs = to_layer_owner(denses[0], denses[1])
    dense = jnp.concatenate([by_core(mine, theirs), by_core(theirs, mine)]).astype(f32)
    dense = dense.reshape(4, -1, features)

    def weight_grad(lefts, rights):
        left_own, left_their = to_layer_owner(*lefts)
        right_own, right_their = to_layer_owner(*rights)
        spec = "jrd,jrf->jdf"
        return jnp.einsum(spec, left_own, right_own, preferred_element_type=f32) + jnp.einsum(
            spec, left_their, right_their, preferred_element_type=f32
        )

    grad_first = weight_grad([k["arrived"] for k in kept], inner_grads)
    grad_second = weight_grad([k["hidden"] for k in kept], backs)
    qkv_grad = dense[:3].reshape(3, -1, HEAD_DIM, features)
    return (
        section_out[None, :, None],
        input_grad[None, :, None],
        small[0:2][None],
        small[2:4][None],
        jnp.transpose(qkv_grad, (0, 3, 1, 2))[None],
        dense[3].reshape(w_attn_out.shape),
        small[8 : 8 + experts].T[None],
        grad_first[None],
        grad_second[None],
    )


def solution(mesh):
    return jax.shard_map(
        per_device,
        mesh=mesh,
        in_specs=(
            P(None, "expert", "tensor", None),
            P(None, "expert", "tensor", None),
            P("section", None, None),
            P("section", None, None),
            P("section", None, None, "tensor", None),
            P("section", "tensor", None, None),
            P("section", None, None),
            P("section", "expert", None, "tensor"),
            P("section", "expert", "tensor", None),
            P("section", None, "expert", None, None),
            P("section", None, "expert", None, None),
        ),
        out_specs=(
            P("section", None, "expert", "tensor", None),
            P("section", None, "expert", "tensor", None),
            P("section", None, None),
            P("section", None, None),
            P("section", None, None, "tensor", None),
            P("section", "tensor", None, None),
            P("section", None, None),
            P("section", "expert", None, "tensor"),
            P("section", "expert", "tensor", None),
        ),
        check_vma=False,
    )
```
